256 devices in a mesh: scen: 16 (over y, x), blk: 16 (over z, core).
Axes of the slice: x: 4, y: 4, z: 8, core: 2. Of those that a mesh axis runs over, the one named last changes fastest.
Arguments:
- link: bfloat16 [64, 256, 4096], P('scen', None, 'blk'), may hold values from -0.15625 to 0.15625
- leaf_inverse: bfloat16 [64, 256, 256], P('scen'), as said below
- leaf_rhs: float32 [64, 256], P('scen'), may hold values from -6 to 6
- node_rhs: float32 [2, 4096], P(None, 'blk'), may hold values from -6 to 6
- node_diag: float32 [2, 4096], P(None, 'blk'), may hold values from 0.5 to 4
- parent: int32 [64], P('scen'), may hold values from 0 to 1
- tile_mask: int32 [64, 16], P('scen', 'blk'), may hold values 0 or 1
Outputs:
- node_solution: float32 [2, 4096], P(None, 'blk')
- leaf_solution: float32 [64, 256], P('scen')
- schur: float32 [2, 4096, 4096], P(None, 'blk', 'scen')
The draws below stay inside these ranges and needn't reach their ends.
Inputs may be any that keep to these rules, and one draw needn't show every extreme that they name: `leaf_inverse`: its diagonal entries lie within 1 to 2.
All inputs are finite; a program needn't handle non-finite values. No bound on the sum of `tile_mask` on one device may be relied on, other than what follows from the above.
Results may differ from the reference program's by a relative error of at most 0.0017.
Values may be sent and summed in bfloat16 or wider, within the bound.
A program may use at most 128 MiB of HBM per device.

```python
import math
import jax
import jax.numpy as jnp
from jax import lax

NP = 4096
NL = 256
NODES = 2
ITERS = 4
LEAVES = 64
TILES = 16


def draw_leaf_inverse(key, part):
    key_off = jax.random.fold_in(key, 11)
    key_diag = jax.random.fold_in(key, 12)
    noise_draw = jax.random.uniform(key_off, (LEAVES, NL, NL), jnp.float32, -1.0, 1.0)
    symmetric = 0.42 * (noise_draw + jnp.swapaxes(noise_draw, 1, 2)) / NL ** 0.5
    leading = jax.random.uniform(key_diag, (LEAVES, NL, 1), jnp.float32, 1.0, 2.0)
    on_diag = lax.broadcasted_iota(jnp.int32, (NL, NL), 0) == lax.broadcasted_iota(jnp.int32, (NL, NL), 1)
    return jnp.where(on_diag[None], leading, symmetric).astype(jnp.bfloat16)


def with_ends(array, rng, least, high):
    spot = [jax.random.randint(jax.random.fold_in(rng, axis), (), 0, length) for axis, length in enumerate(array.shape)]
    longest = array.shape.index(max(array.shape))
    neighbour = spot[:longest] + [(spot[longest] + 1) % array.shape[longest]] + spot[longest + 1:]
    return array.at[tuple(spot)].set(least).at[tuple(neighbour)].set(high)


def block_levels(stream_key, extent, pieces, low, largest):
    level, own = 1.0, jax.random.fold_in(stream_key, 6)
    for axis_at, shards_of in pieces:
        steps = jnp.exp(jax.random.uniform(jax.random.fold_in(own, axis_at), (shards_of,), jnp.float32, low / len(pieces), largest / len(pieces)))
        level = level * jnp.repeat(steps, extent[axis_at] // shards_of).reshape([-1 if axis == axis_at else 1 for axis in range(len(extent))])
    return level


def centred(rng, dims, width, most, shards=(), held_as=jnp.bfloat16):
    values = width * jax.random.normal(rng, dims, jnp.float32)
    if shards:
        values = values * block_levels(rng, dims, shards, -0.22, 0.18)
    return jnp.clip(values, -most, most).astype(held_as)


def setup_inputs(seed: int = 0) -> dict:
    keys = jax.random.split(jax.random.key(seed), 8)
    link = centred(keys[0], (LEAVES, NL, NP), (NL * LEAVES // NODES // 6) ** -0.5, 0.15625, ((0, 16), (2, 16)))
    leaf_inverse = draw_leaf_inverse(jax.random.fold_in(keys[7], 71), 0)
    leaf_rhs = centred(keys[2], (LEAVES, NL), 1.0, 6.0, ((0, 16),), jnp.float32)
    node_rhs = centred(keys[3], (NODES, NP), 1.0, 6.0, ((1, 16),), jnp.float32)
    node_diag = jnp.clip(jnp.exp(math.log(4.0) - 2.0794415 * jax.random.uniform(keys[4], (NODES, NP), jnp.float32) ** block_levels(keys[4], (NODES, NP), ((1, 16),), -0.2, 0.2)), 0.5, 4.0)
    parent = with_ends(jax.random.randint(keys[5], (LEAVES,), 0, NODES), jax.random.fold_in(keys[5], 1), 0, NODES - 1).astype(jnp.int32)
    tile_mask = with_ends((jax.random.randint(keys[6], (LEAVES, TILES), 0, 2) < 1).astype(jnp.int32), jax.random.fold_in(keys[6], 1), 0, 1)
    return {"link": link, "leaf_inverse": leaf_inverse, "leaf_rhs": leaf_rhs, "node_rhs": node_rhs, "node_diag": node_diag, "parent": parent, "tile_mask": tile_mask}


highest = lax.Precision.HIGHEST
damping = 0.4


def reference(link, leaf_inverse, leaf_rhs, node_rhs, node_diag, parent, tile_mask):
    leaf_count, width_leaf, full_width = link.shape
    node_count = node_rhs.shape[0]
    tile_count = tile_mask.shape[1]
    tile_width = full_width // tile_count
    column_mask = jnp.repeat(tile_mask.astype(jnp.bfloat16), tile_width, axis=1)
    masked = link * column_mask[:, None, :]
    inverse_f = leaf_inverse.astype(jnp.float32)
    masked_f = masked.astype(jnp.float32)
    solved = jnp.einsum("lnm,lmc->lnc", inverse_f, masked_f, precision=highest).astype(jnp.bfloat16)

    def accumulate(carry, items):
        link_rows, solved_rows, owner = items
        update = jnp.dot(link_rows.astype(jnp.float32).T, solved_rows.astype(jnp.float32), precision=highest)
        return carry.at[owner].add(update), None

    start_blocks = jnp.zeros((node_count, full_width, full_width), jnp.float32)
    schur, unused = lax.scan(accumulate, start_blocks, (masked, solved, parent))
    ownership = (parent[:, None] == jnp.arange(node_count, dtype=jnp.int32)[None, :]).astype(jnp.float32)
    leaf_solve = jnp.einsum("lnm,lm->ln", inverse_f, leaf_rhs, precision=highest)
    leaf_terms = jnp.einsum("lnc,ln->lc", masked_f, leaf_solve, precision=highest)
    reduced = node_rhs - jnp.dot(ownership.T, leaf_terms, precision=highest)
    scaling = node_diag + jnp.diagonal(schur, axis1=1, axis2=2)
    current = reduced / scaling
    for sweep in range(ITERS):
        product = node_diag * current + jnp.einsum("prc,pc->pr", schur, current, precision=highest)
        current = current + damping * (reduced - product) / scaling
    parent_values = jnp.dot(ownership, current, precision=highest)
    coupling = jnp.einsum("lnc,lc->ln", masked_f, parent_values, precision=highest)
    leaf_solution = jnp.einsum("lnm,lm->ln", inverse_f, leaf_rhs - coupling, precision=highest)
    return current, leaf_solution, schur
```

```python
import functools

import jax
import jax.numpy as jnp
from jax import lax
from jax.experimental import pallas as pl
from jax.experimental.pallas import tpu as pltpu
from jax.sharding import PartitionSpec as P

ITERS = 4
DAMPING = 0.4
MESH = pl.DeviceIdType.MESH
F32 = jnp.float32
BF16 = jnp.bfloat16


def split_rows(v):
    hi = v.astype(BF16).astype(F32)
    rest = v - hi
    mid = rest.astype(BF16).astype(F32)
    low = rest - mid
    return jnp.concatenate([hi, mid, low, jnp.zeros_like(v)], axis=0).astype(BF16)


def leaf_products(v, mats_ref, contract):
    parts = split_rows(v)
    leaves = mats_ref.shape[0]
    row = lax.broadcasted_iota(jnp.int32, v.shape, 0)
    total = jnp.zeros(v.shape, F32)
    for leaf in range(leaves):
        out = lax.dot_general(
            parts, mats_ref[leaf], (((1,), (contract,)), ((), ())), preferred_element_type=F32
        )
        out = out[0:4] + out[4:8] + out[8:12]
        total = total + jnp.where(row == leaf, out, 0.0)
    return total


def solve_kernel(
    scens, blks,
    parent_ref, mask_ref, link_ref, inv_ref, rhs_ref, nrhs_ref, ndiag_ref,
    node_ref, leaf_ref,
    masked, solved, first, tbuf, ubuf, send_sem, recv_sem,
):
    scen = lax.axis_index("scen")
    blk = lax.axis_index("blk")
    leaves = link_ref.shape[0]
    barrier = pltpu.get_barrier_semaphore()
    for d in range(1, blks):
        pl.semaphore_signal(barrier, inc=1, device_id=(scen, lax.rem(blk + d, blks)), device_id_type=MESH)
    for d in range(1, scens):
        pl.semaphore_signal(barrier, inc=1, device_id=(lax.rem(scen + d, scens), blk), device_id_type=MESH)

    for leaf in range(leaves):
        m = link_ref[leaf] * mask_ref[leaf].astype(BF16)
        masked[leaf] = m
        solved[leaf] = jnp.dot(inv_ref[leaf], m, preferred_element_type=F32).astype(BF16)

    owner = [parent_ref[leaf].astype(F32) for leaf in range(leaves)]
    row2 = lax.broadcasted_iota(jnp.int32, nrhs_ref.shape, 0)
    row4 = lax.broadcasted_iota(jnp.int32, rhs_ref.shape, 0)

    def by_parent(rows):
        total = jnp.zeros(nrhs_ref.shape, F32)
        for leaf in range(leaves):
            weight = jnp.where(row2 == 0, 1.0 - owner[leaf], owner[leaf])
            total = total + weight * rows[leaf : leaf + 1]
        return total

    def of_parent(values):
        total = jnp.zeros(rhs_ref.shape, F32)
        for leaf in range(leaves):
            mine = values[0:1] * (1.0 - owner[leaf]) + values[1:2] * owner[leaf]
            total = total + jnp.where(row4 == leaf, mine, 0.0)
        return total

    def send(buf, index, value, over, me, count):
        buf[me] = value
        for d in range(1, count):
            peer = lax.rem(me + d, count)
            target = (scen, peer) if over == "blk" else (peer, blk)
            pltpu.make_async_remote_copy(
                src_ref=buf.at[me], dst_ref=buf.at[me],
                send_sem=send_sem.at[index], recv_sem=recv_sem.at[index],
                device_id=target, device_id_type=MESH,
            ).start()

    def collect(buf, index, count):
        rest = buf.at[pl.ds(0, count - 1)]
        pltpu.make_async_copy(rest, rest, recv_sem.at[index]).wait()
        total = buf[0]
        for j in range(1, count):
            total = total + buf[j]
        return total

    def drain(buf, index, count):
        rest = buf.at[pl.ds(0, count - 1)]
        pltpu.make_async_copy(rest, rest, send_sem.at[index]).wait()

    leaf_rhs = rhs_ref[...]
    leaf_solve = leaf_products(leaf_rhs, inv_ref, 1)
    rhs_terms = by_parent(leaf_products(leaf_solve, masked, 0))
    diag_rows = jnp.concatenate(
        [
            jnp.sum(masked[leaf].astype(F32) * solved[leaf].astype(F32), axis=0, keepdims=True)
            for leaf in range(leaves)
        ],
        axis=0,
    )
    diag_terms = by_parent(diag_rows)
    pl.semaphore_wait(barrier, (blks - 1) + (scens - 1))

    send(first, 0, jnp.concatenate([rhs_terms, diag_terms], axis=0), "scen", scen, scens)
    sums = collect(first, 0, scens)
    node_diag = ndiag_ref[...]
    reduced = nrhs_ref[...] - sums[0:2]
    scaling = node_diag + sums[2:4]
    x = reduced / scaling
    for it in range(ITERS):
        send(tbuf.at[it], 1 + it, leaf_products(of_parent(x), solved, 1), "blk", blk, blks)
        inner = collect(tbuf.at[it], 1 + it, blks)
        send(ubuf.at[it], 6 + it, by_parent(leaf_products(inner, masked, 0)), "scen", scen, scens)
        product = node_diag * x + collect(ubuf.at[it], 6 + it, scens)
        x = x + DAMPING * (reduced - product) / scaling
    node_ref[...] = x
    send(tbuf.at[ITERS], 1 + ITERS, leaf_products(of_parent(x), masked, 1), "blk", blk, blks)
    coupling = collect(tbuf.at[ITERS], 1 + ITERS, blks)
    leaf_ref[...] = leaf_products(leaf_rhs - coupling, inv_ref, 1)

    drain(first, 0, scens)
    for it in range(ITERS + 1):
        drain(tbuf.at[it], 1 + it, blks)
    for it in range(ITERS):
        drain(ubuf.at[it], 6 + it, scens)


def body(link, leaf_inverse, leaf_rhs, node_rhs, node_diag, parent, tile_mask):
    leaf_count, width_leaf, tile_width = link.shape
    node_count = node_rhs.shape[0]
    scens = lax.axis_size("scen")
    blks = lax.axis_size("blk")
    vmem = pl.BlockSpec(memory_space=pltpu.VMEM)
    smem = pl.BlockSpec(memory_space=pltpu.SMEM)
    node_solution, leaf_solution = pl.pallas_call(
        functools.partial(solve_kernel, scens, blks),
        out_shape=(
            jax.ShapeDtypeStruct((node_count, tile_width), F32),
            jax.ShapeDtypeStruct((leaf_count, width_leaf), F32),
        ),
        in_specs=[smem, smem] + [vmem] * 5,
        out_specs=(vmem, vmem),
        scratch_shapes=[
            pltpu.VMEM((leaf_count, width_leaf, tile_width), BF16),
            pltpu.VMEM((leaf_count, width_leaf, tile_width), BF16),
            pltpu.VMEM((scens, 2 * node_count, tile_width), F32),
            pltpu.VMEM((ITERS + 1, blks, leaf_count, width_leaf), F32),
            pltpu.VMEM((ITERS, scens, node_count, tile_width), F32),
            pltpu.SemaphoreType.DMA((10,)),
            pltpu.SemaphoreType.DMA((10,)),
        ],
        compiler_params=pltpu.CompilerParams(collective_id=0, has_side_effects=True),
        name="solve",
    )(parent, tile_mask.reshape(-1), link, leaf_inverse, leaf_rhs, node_rhs, node_diag)

    masked = link * tile_mask.astype(BF16)[:, :, None]
    solved = jnp.einsum("lnm,lmc->lnc", leaf_inverse, masked, preferred_element_type=F32).astype(BF16)
    node_ids = lax.broadcasted_iota(jnp.int32, (leaf_count, node_count), 1)
    member = (parent[:, None] == node_ids).astype(BF16)
    chosen = masked[None] * member.T[:, :, None, None]
    chosen = chosen.reshape(node_count, leaf_count * width_leaf, tile_width)
    stacked = lax.all_gather(solved.reshape(leaf_count * width_leaf, tile_width), "blk", axis=0)
    partial_value = jnp.einsum("pkr,skc->sprc", chosen, stacked, preferred_element_type=F32)
    schur_out = lax.psum_scatter(partial_value, "scen", scatter_dimension=0, tiled=False)
    return (node_solution, leaf_solution, schur_out)


def solution(mesh):
    in_specs = (
        P("scen", None, "blk"),
        P("scen", None, None),
        P("scen", None),
        P(None, "blk"),
        P(None, "blk"),
        P("scen"),
        P("scen", "blk"),
    )
    out_specs = (P(None, "blk"), P("scen", None), P(None, "blk", "scen"))
    return jax.shard_map(body, mesh=mesh, in_specs=in_specs, out_specs=out_specs, check_vma=False)
```

```python
import functools

import jax
import jax.numpy as jnp
from jax import lax
from jax.experimental import pallas as pl
from jax.experimental.pallas import tpu as pltpu
from jax.sharding import PartitionSpec as P

ITERS = 4
DAMPING = 0.4
MESH = pl.DeviceIdType.MESH
F32 = jnp.float32
BF16 = jnp.bfloat16


def split_rows(v):
    hi = v.astype(BF16).astype(F32)
    rest = v - hi
    mid = rest.astype(BF16).astype(F32)
    low = rest - mid
    return jnp.concatenate([hi, mid, low, jnp.zeros_like(v)], axis=0).astype(BF16)


def leaf_products(v, mats_ref, contract):
    parts = split_rows(v)
    leaves = mats_ref.shape[0]
    row = lax.broadcasted_iota(jnp.int32, v.shape, 0)
    total = jnp.zeros(v.shape, F32)
    for leaf in range(leaves):
        out = lax.dot_general(
            parts, mats_ref[leaf], (((1,), (contract,)), ((), ())), preferred_element_type=F32
        )
        out = out[0:4] + out[4:8] + out[8:12]
        total = total + jnp.where(row == leaf, out, 0.0)
    return total


def solve_kernel(
    scens, blks,
    parent_ref, mask_ref, link_ref, inv_ref, rhs_ref, nrhs_ref, ndiag_ref,
    node_ref, leaf_ref,
    masked, solved, first, tbuf, ubuf, send_sem, recv_sem,
):
    scen = lax.axis_index("scen")
    blk = lax.axis_index("blk")
    leaves = link_ref.shape[0]
    barrier = pltpu.get_barrier_semaphore()
    for d in range(1, blks):
        pl.semaphore_signal(barrier, inc=1, device_id=(scen, lax.rem(blk + d, blks)), device_id_type=MESH)
    for d in range(1, scens):
        pl.semaphore_signal(barrier, inc=1, device_id=(lax.rem(scen + d, scens), blk), device_id_type=MESH)

    for leaf in range(leaves):
        m = link_ref[leaf] * mask_ref[leaf].astype(BF16)
        masked[leaf] = m
        solved[leaf] = jnp.dot(inv_ref[leaf], m, preferred_element_type=F32).astype(BF16)

    owner = [parent_ref[leaf].astype(F32) for leaf in range(leaves)]
    row2 = lax.broadcasted_iota(jnp.int32, nrhs_ref.shape, 0)
    row4 = lax.broadcasted_iota(jnp.int32, rhs_ref.shape, 0)

    def by_parent(rows):
        total = jnp.zeros(nrhs_ref.shape, F32)
        for leaf in range(leaves):
            weight = jnp.where(row2 == 0, 1.0 - owner[leaf], owner[leaf])
            total = total + weight * rows[leaf : leaf + 1]
        return total

    def of_parent(values):
        total = jnp.zeros(rhs_ref.shape, F32)
        for leaf in range(leaves):
            mine = values[0:1] * (1.0 - owner[leaf]) + values[1:2] * owner[leaf]
            total = total + jnp.where(row4 == leaf, mine, 0.0)
        return total

    def send(buf, index, value, over, me, count):
        buf[me] = value
        for d in range(1, count):
            peer = lax.rem(me + d, count)
            target = (scen, peer) if over == "blk" else (peer, blk)
            pltpu.make_async_remote_copy(
                src_ref=buf.at[me], dst_ref=buf.at[me],
                send_sem=send_sem.at[index], recv_sem=recv_sem.at[index],
                device_id=target, device_id_type=MESH,
            ).start()

    def collect(buf, index, count):
        rest = buf.at[pl.ds(0, count - 1)]
        pltpu.make_async_copy(rest, rest, recv_sem.at[index]).wait()
        total = buf[0]
        for j in range(1, count):
            total = total + buf[j]
        return total

    def drain(buf, index, count):
        rest = buf.at[pl.ds(0, count - 1)]
        pltpu.make_async_copy(rest, rest, send_sem.at[index]).wait()

    leaf_rhs = rhs_ref[...]
    leaf_solve = leaf_products(leaf_rhs, inv_ref, 1)
    rhs_terms = by_parent(leaf_products(leaf_solve, masked, 0))
    diag_rows = jnp.concatenate(
        [
            jnp.sum(masked[leaf].astype(F32) * solved[leaf].astype(F32), axis=0, keepdims=True)
            for leaf in range(leaves)
        ],
        axis=0,
    )
    diag_terms = by_parent(diag_rows)
    pl.semaphore_wait(barrier, (blks - 1) + (scens - 1))

    send(first, 0, jnp.concatenate([rhs_terms, diag_terms], axis=0), "scen", scen, scens)
    sums = collect(first, 0, scens)
    node_diag = ndiag_ref[...]
    reduced = nrhs_ref[...] - sums[0:2]
    scaling = node_diag + sums[2:4]
    x = reduced / scaling
    for it in range(ITERS):
        send(tbuf.at[it], 1 + it, leaf_products(of_parent(x), solved, 1), "blk", blk, blks)
        inner = collect(tbuf.at[it], 1 + it, blks)
        send(ubuf.at[it], 6 + it, by_parent(leaf_products(inner, masked, 0)), "scen", scen, scens)
        product = node_diag * x + collect(ubuf.at[it], 6 + it, scens)
        x = x + DAMPING * (reduced - product) / scaling
    node_ref[...] = x
    send(tbuf.at[ITERS], 1 + ITERS, leaf_products(of_parent(x), masked, 1), "blk", blk, blks)
    coupling = collect(tbuf.at[ITERS], 1 + ITERS, blks)
    leaf_ref[...] = leaf_products(leaf_rhs - coupling, inv_ref, 1)

    drain(first, 0, scens)
    for it in range(ITERS + 1):
        drain(tbuf.at[it], 1 + it, blks)
    for it in range(ITERS):
        drain(ubuf.at[it], 6 + it, scens)


XS = 4
ZS = 8


def schur_kernel(
    parent_ref, mask_ref, link_ref, inv_ref, out_ref,
    own, sbuf, mraw, weight, mboth, obuf, orecv,
    a_send, a_recv, m_send, m_recv, w_send, w_recv, z_send, z_recv,
    p_send, p_recv, q_recv, o_send, o_recv,
):
    scen = lax.axis_index("scen")
    blk = lax.axis_index("blk")
    y, x = scen // XS, lax.rem(scen, XS)
    z, c = blk // 2, lax.rem(blk, 2)
    leaves, width, cols = link_ref.shape
    half = cols // 2
    source = lax.rem(z, 2) == x // 2
    partner = (scen, 2 * z + 1 - c)

    barrier = pltpu.get_barrier_semaphore()

    def greet(s, b):
        pl.semaphore_signal(barrier, inc=1, device_id=(s, b), device_id_type=MESH)

    for d in range(XS):
        for e in range(2):
            if d or e:
                greet(XS * y + lax.rem(x + d, XS), 2 * z + lax.rem(c + e, 2))
    for d in range(1, 4):
        greet(XS * lax.rem(y + d, 4) + x, blk)
    for d in (1, ZS - 1):
        greet(scen, 2 * lax.rem(z + d, ZS) + c)

    for leaf in range(leaves):
        m = link_ref[leaf] * mask_ref[leaf].astype(BF16)
        s = jnp.dot(inv_ref[leaf], m, preferred_element_type=F32).astype(BF16)
        for h in range(2):
            own[h, leaf * width : (leaf + 1) * width, :] = s[:, h * half : (h + 1) * half]
        mraw[x, :, leaf * width : (leaf + 1) * width] = m.astype(F32).T.astype(BF16)
    weight[x] = jnp.concatenate(
        [jnp.full((1, 128), parent_ref[leaf].astype(F32), F32) for leaf in range(leaves)]
        + [jnp.zeros((8 - leaves, 128), F32)],
        axis=0,
    )
    pl.semaphore_wait(barrier, 7 + 3 + 2)

    def piece(m, h, k):
        return (m * 2 + h) * XS + k

    to_x = 2 * lax.rem(z, 2) + c
    lane = x // 2
    itself = jnp.logical_and(to_x == x, lane == c)
    for first in range(2):
        h = lax.rem(x + first, 2)
        place = piece(z // 2, h, x)
        slot = a_recv.at[h, lax.rem(x, 2)]

        @pl.when(itself)
        def _():
            pltpu.make_async_copy(own.at[h], sbuf.at[place], slot).start()

        @pl.when(jnp.logical_not(itself))
        def _():
            pltpu.make_async_remote_copy(
                src_ref=own.at[h], dst_ref=sbuf.at[place], send_sem=a_send, recv_sem=slot,
                device_id=(XS * y + to_x, 2 * z + lane), device_id_type=MESH,
            ).start()

    for d in (1, 3, 2):
        peer = (XS * y + lax.rem(x + d, XS), blk)
        pltpu.make_async_remote_copy(
            src_ref=weight.at[x], dst_ref=weight.at[x], send_sem=w_send, recv_sem=w_recv.at[x],
            device_id=peer, device_id_type=MESH,
        ).start()
        pltpu.make_async_remote_copy(
            src_ref=mraw.at[x], dst_ref=mraw.at[x], send_sem=m_send, recv_sem=m_recv.at[x],
            device_id=peer, device_id_type=MESH,
        ).start()

    def ring(direction, place, step):
        pltpu.make_async_remote_copy(
            src_ref=sbuf.at[place], dst_ref=sbuf.at[place],
            send_sem=z_send.at[direction], recv_sem=z_recv.at[direction, step],
            device_id=(scen, 2 * lax.rem(z + (1 if direction == 0 else ZS - 1), ZS) + c), device_id_type=MESH,
        ).start()

    def share(place, slot):
        pltpu.make_async_remote_copy(
            src_ref=sbuf.at[place], dst_ref=sbuf.at[place], send_sem=p_send, recv_sem=slot,
            device_id=partner, device_id_type=MESH,
        ).start()

    def arrived(place, slot):
        pltpu.make_async_copy(sbuf.at[place], sbuf.at[place], slot).wait()

    mine = z // 2

    @pl.when(source)
    def _():
        def have(h, kk):
            place = piece(mine, h, 2 * c + kk)
            arrived(place, a_recv.at[h, kk])
            share(place, q_recv.at[h, kk])
            return place

        p00 = have(0, 0)
        ring(0, p00, 0)
        p11 = have(1, 1)
        ring(1, p11, 0)
        p10 = have(1, 0)
        ring(1, p10, 1)
        p01 = have(0, 1)
        ring(0, p01, 1)
        ring(0, p10, 2)
        ring(1, p01, 2)
        ring(0, p11, 3)
        ring(1, p00, 3)

    base = jnp.where(source, 2, 1)

    def group(direction, i):
        away = base + 2 * (i // 2)
        at = lax.rem(z + ZS - away, ZS) if direction == 0 else lax.rem(z + away, ZS)
        h = lax.rem(i, 2)
        return at // 2, (h if direction == 0 else 1 - h)

    def step(direction, i, e):
        m, h = group(direction, i)
        place = piece(m, h, 2 * c + (e if direction == 0 else 1 - e))
        t = 2 * i + e
        arrived(place, z_recv.at[direction, t])

        @pl.when(jnp.where(source, i < 2, i < 3))
        def _():
            ring(direction, place, t + jnp.where(source, 4, 0))

        share(place, p_recv.at[direction, t])

    def product(m, h):
        def over(k, total):
            return total + jnp.dot(mboth[k], sbuf[piece(m, h, k)], preferred_element_type=F32)

        obuf[m * 2 + h] = lax.fori_loop(0, XS, over, jnp.zeros((2 * cols, half), F32))

        @pl.when(m != y)
        def _():
            pltpu.make_async_remote_copy(
                src_ref=obuf.at[m * 2 + h], dst_ref=orecv.at[y * 2 + h],
                send_sem=o_send, recv_sem=o_recv.at[y, h],
                device_id=(XS * m + x, blk), device_id_type=MESH,
            ).start()

    def finish(direction, i):
        m, h = group(direction, i)
        for e in range(2):
            place = piece(m, h, 2 * (1 - c) + (e if direction == 0 else 1 - e))
            arrived(place, p_recv.at[direction, 2 * i + e])
        product(m, h)

    def early(i, carry):
        for e in range(2):
            for direction in range(2):
                step(direction, i, e)
        return carry

    lax.fori_loop(0, 2, early, 0)

    for d in range(1, XS):
        other = lax.rem(x + d, XS)
        pltpu.make_async_copy(weight.at[other], weight.at[other], w_recv.at[other]).wait()
        pltpu.make_async_copy(mraw.at[other], mraw.at[other], m_recv.at[other]).wait()

    def both(k, carry):
        w = weight[k]
        row = jnp.concatenate([w[leaf : leaf + 1] for leaf in range(leaves) for _ in range(width // 128)], axis=1)
        raw = mraw[k].astype(F32)
        mboth[k, :cols, :] = (raw * (1.0 - row)).astype(BF16)
        mboth[k, cols:, :] = (raw * row).astype(BF16)
        return carry

    lax.fori_loop(0, XS, both, 0)

    @pl.when(source)
    def _():
        def one(h, carry):
            for kk in range(2):
                arrived(piece(mine, h, 2 * (1 - c) + kk), q_recv.at[h, kk])
            product(mine, h)
            return carry

        lax.fori_loop(0, 2, one, 0)

    def settle(i, carry):
        finish(0, i)
        finish(1, i)
        return carry

    lax.fori_loop(0, 2, settle, 0)

    def late(i, carry):
        @pl.when(jnp.logical_or(jnp.logical_not(source), i < 3))
        def _():
            for e in range(2):
                for direction in range(2):
                    step(direction, i, e)
            finish(0, i)
            finish(1, i)

        return carry

    lax.fori_loop(2, 4, late, 0)

    for d in range(1, 4):
        other = lax.rem(y + d, 4)
        for h in range(2):
            pltpu.make_async_copy(orecv.at[other * 2 + h], orecv.at[other * 2 + h], o_recv.at[other, h]).wait()
    for h in range(2):
        total = obuf[y * 2 + h]
        for d in range(1, 4):
            total = total + orecv[lax.rem(y + d, 4) * 2 + h]
        out_ref[0, :, h * half : (h + 1) * half] = total[:cols]
        out_ref[1, :, h * half : (h + 1) * half] = total[cols:]

    def drain(ref, count, sem):
        pltpu.make_async_copy(ref.at[pl.ds(0, count)], ref.at[pl.ds(0, count)], sem).wait()

    @pl.when(jnp.logical_not(itself))
    def _():
        drain(sbuf, 2, a_send)

    drain(weight, 3, w_send)
    drain(mraw, 3, m_send)
    for direction in range(2):

        @pl.when(source)
        def _():
            drain(sbuf, 8, z_send.at[direction])

        @pl.when(jnp.logical_not(source))
        def _():
            drain(sbuf, 6, z_send.at[direction])

    drain(sbuf, 16, p_send)
    drain(obuf, 6, o_send)


def schur_call(parent, tile_mask, link, leaf_inverse):
    leaves, width, cols = link.shape
    vmem = pl.BlockSpec(memory_space=pltpu.VMEM)
    smem = pl.BlockSpec(memory_space=pltpu.SMEM)
    dma = pltpu.SemaphoreType.DMA
    return pl.pallas_call(
        schur_kernel,
        out_shape=jax.ShapeDtypeStruct((2, cols, cols), F32),
        in_specs=[smem, smem, vmem, vmem],
        out_specs=vmem,
        scratch_shapes=[
            pltpu.VMEM((2, leaves * width, cols // 2), BF16),
            pltpu.VMEM((8 * XS, leaves * width, cols // 2), BF16),
            pltpu.VMEM((XS, cols, leaves * width), BF16),
            pltpu.VMEM((XS, 8, 128), F32),
            pltpu.VMEM((XS, 2 * cols, leaves * width), BF16),
            pltpu.VMEM((8, 2 * cols, cols // 2), F32),
            pltpu.VMEM((8, 2 * cols, cols // 2), F32),
            dma, dma((2, 2)), dma, dma((XS,)), dma, dma((XS,)), dma((2,)), dma((2, 8)),
            dma, dma((2, 8)), dma((2, 2)), dma, dma((4, 2)),
        ],
        compiler_params=pltpu.CompilerParams(collective_id=1, has_side_effects=True, vmem_limit_bytes=60000 * 1024),
        name="schur",
    )(parent, tile_mask, link, leaf_inverse)


def body(link, leaf_inverse, leaf_rhs, node_rhs, node_diag, parent, tile_mask):
    leaf_count, width_leaf, tile_width = link.shape
    node_count = node_rhs.shape[0]
    scens = lax.axis_size("scen")
    blks = lax.axis_size("blk")
    vmem = pl.BlockSpec(memory_space=pltpu.VMEM)
    smem = pl.BlockSpec(memory_space=pltpu.SMEM)
    node_solution, leaf_solution = pl.pallas_call(
        functools.partial(solve_kernel, scens, blks),
        out_shape=(
            jax.ShapeDtypeStruct((node_count, tile_width), F32),
            jax.ShapeDtypeStruct((leaf_count, width_leaf), F32),
        ),
        in_specs=[smem, smem] + [vmem] * 5,
        out_specs=(vmem, vmem),
        scratch_shapes=[
            pltpu.VMEM((leaf_count, width_leaf, tile_width), BF16),
            pltpu.VMEM((leaf_count, width_leaf, tile_width), BF16),
            pltpu.VMEM((scens, 2 * node_count, tile_width), F32),
            pltpu.VMEM((ITERS + 1, blks, leaf_count, width_leaf), F32),
            pltpu.VMEM((ITERS, scens, node_count, tile_width), F32),
            pltpu.SemaphoreType.DMA((10,)),
            pltpu.SemaphoreType.DMA((10,)),
        ],
        compiler_params=pltpu.CompilerParams(collective_id=0, has_side_effects=True),
        name="solve",
    )(parent, tile_mask.reshape(-1), link, leaf_inverse, leaf_rhs, node_rhs, node_diag)

    schur_out = schur_call(parent, tile_mask.reshape(-1), link, leaf_inverse)
    return (node_solution, leaf_solution, schur_out)


def solution(mesh):
    in_specs = (
        P("scen", None, "blk"),
        P("scen", None, None),
        P("scen", None),
        P(None, "blk"),
        P(None, "blk"),
        P("scen"),
        P("scen", "blk"),
    )
    out_specs = (P(None, "blk"), P("scen", None), P(None, "blk", "scen"))
    return jax.shard_map(body, mesh=mesh, in_specs=in_specs, out_specs=out_specs, check_vma=False)
```

```python
import jax
import jax.numpy as jnp
from jax import lax
from jax.experimental import pallas as pl
from jax.experimental.pallas import tpu as pltpu
from jax.sharding import PartitionSpec as P

ITERS = 4
DAMPING = 0.4
MESH = pl.DeviceIdType.MESH
F32 = jnp.float32
BF16 = jnp.bfloat16
XS = 4
YS = 4
ZS = 8
SCENS = XS * YS


def split_rows(v):
    hi = v.astype(BF16).astype(F32)
    rest = v - hi
    mid = rest.astype(BF16).astype(F32)
    low = rest - mid
    return jnp.concatenate([hi, mid, low, jnp.zeros_like(v)], axis=0).astype(BF16)


def leaf_products(v, mats_ref, contract):
    parts = split_rows(v)
    leaves = mats_ref.shape[0]
    row = lax.broadcasted_iota(jnp.int32, v.shape, 0)
    total = jnp.zeros(v.shape, F32)
    for leaf in range(leaves):
        out = lax.dot_general(
            parts, mats_ref[leaf], (((1,), (contract,)), ((), ())), preferred_element_type=F32
        )
        out = out[0:4] + out[4:8] + out[8:12]
        total = total + jnp.where(row == leaf, out, 0.0)
    return total


def step_kernel(
    parent_ref, mask_ref, link_ref, inv_ref, rhs_ref, nrhs_ref, ndiag_ref,
    node_ref, leaf_ref, out_ref,
    masked, solved, first, ubuf, tbuf, pair,
    own, sbuf, mraw, weight, mboth, obuf, orecv,
    f_send, f_recv, u_send, u_recv, t_send, t_recv, c_send, c_recv,
    a_send, a_recv, m_send, m_recv, w_send, w_recv, z_send, z_recv,
    p_send, p_recv, q_recv, o_send, o_recv,
):
    scen = lax.axis_index("scen")
    blk = lax.axis_index("blk")
    y, x = scen // XS, lax.rem(scen, XS)
    z, c = blk // 2, lax.rem(blk, 2)
    leaves, width, cols = link_ref.shape
    half = cols // 2
    source = lax.rem(z, 2) == x // 2
    partner = (scen, 2 * z + 1 - c)
    barrier = pltpu.get_barrier_semaphore()

    def greet(s, b):
        pl.semaphore_signal(barrier, inc=1, device_id=(s, b), device_id_type=MESH)

    for d in range(1, ZS):
        for e in range(2):
            greet(scen, 2 * lax.rem(z + d, ZS) + e)
    for d in range(1, SCENS):
        greet(lax.rem(scen + d, SCENS), blk)
    for d in range(XS):
        greet(XS * y + lax.rem(x + d, XS), 2 * z + 1 - c)

    def put(src, dst, send, recv, target):
        pltpu.make_async_remote_copy(
            src_ref=src, dst_ref=dst, send_sem=send, recv_sem=recv, device_id=target, device_id_type=MESH
        ).start()

    def wait(ref, sem):
        pltpu.make_async_copy(ref, ref, sem).wait()

    for leaf in range(leaves):
        m = link_ref[leaf] * mask_ref[leaf].astype(BF16)
        s = jnp.dot(inv_ref[leaf], m, preferred_element_type=F32).astype(BF16)
        masked[leaf] = m
        solved[leaf] = s
        for h in range(2):
            own[h, leaf * width : (leaf + 1) * width, :] = s[:, h * half : (h + 1) * half]
        mraw[x, leaf] = m.astype(F32).T.astype(BF16)
    owner = [parent_ref[leaf].astype(F32) for leaf in range(leaves)]
    weight[x] = jnp.concatenate(
        [jnp.full((1, 128), owner[leaf], F32) for leaf in range(leaves)] + [jnp.zeros((8 - leaves, 128), F32)],
        axis=0,
    )

    row2 = lax.broadcasted_iota(jnp.int32, nrhs_ref.shape, 0)
    row4 = lax.broadcasted_iota(jnp.int32, rhs_ref.shape, 0)

    def by_parent(rows):
        total = jnp.zeros(nrhs_ref.shape, F32)
        for leaf in range(leaves):
            share_of = jnp.where(row2 == 0, 1.0 - owner[leaf], owner[leaf])
            total = total + share_of * rows[leaf : leaf + 1]
        return total

    def of_parent(values):
        total = jnp.zeros(rhs_ref.shape, F32)
        for leaf in range(leaves):
            mine = values[0:1] * (1.0 - owner[leaf]) + values[1:2] * owner[leaf]
            total = total + jnp.where(row4 == leaf, mine, 0.0)
        return total

    def scen_send(buf, value, send, recv):
        buf[scen] = value
        for d in range(1, SCENS):
            put(buf.at[scen], buf.at[scen], send, recv, (lax.rem(scen + d, SCENS), blk))

    def collect(buf, recv, count):
        wait(buf.at[pl.ds(0, count - 1)], recv)
        total = buf[0]
        for j in range(1, count):
            total = total + buf[j]
        return total

    def blk_begin(it, value):
        pair[it, c] = value
        put(pair.at[it, c], pair.at[it, c], c_send, c_recv.at[it], partner)

    def blk_send(it):
        wait(pair.at[it, 0], c_recv.at[it])
        at = ZS * it + z
        tbuf[at] = pair[it, 0] + pair[it, 1]
        for d in range(1, ZS // 2 + 1):
            to = lax.rem(z + jnp.where(c == 0, ZS - d, d), ZS)

            def both_cores():
                for e in range(2):
                    put(tbuf.at[at], tbuf.at[at], t_send, t_recv.at[it], (scen, 2 * to + e))

            if d < ZS // 2:
                both_cores()
            else:
                pl.when(lax.rem(z + c, 2) == 1)(both_cores)

    def blk_collect(it):
        return collect(tbuf.at[pl.ds(ZS * it, ZS)], t_recv.at[it], ZS)

    def u_at(it):
        return ubuf.at[pl.ds(SCENS * it, SCENS)]

    def piece(m, h, k):
        return (m * 2 + h) * XS + k

    def ring(place, step):
        to = lax.rem(z + jnp.where(c == 0, 1, ZS - 1), ZS)
        put(sbuf.at[place], sbuf.at[place], z_send, z_recv.at[step], (scen, 2 * to + c))

    def share(place, slot):
        put(sbuf.at[place], sbuf.at[place], p_send, slot, partner)

    mine = z // 2

    def order(q):
        return q // 4, lax.rem(2 * c + lax.rem(q, 4), 4)

    def own_piece(q):
        h, k = order(q)
        return piece(mine, h, k)

    def start_own(h):
        @pl.when(source)
        def _():
            for e in range(2):
                place = own_piece(4 * h + e)
                wait(sbuf.at[place], a_recv.at[h, e])
                share(place, q_recv.at[h, e])
                ring(place, 4 * h + e)

    def start_other(h):
        @pl.when(source)
        def _():
            for e in range(2):
                place = own_piece(4 * h + 2 + e)
                wait(sbuf.at[place], q_recv.at[h, e])
                ring(place, 4 * h + 2 + e)

    def extra(g):
        return g == 2 + c

    def serve(plain_range, source_range):
        begin = jnp.where(source, source_range[0], plain_range[0])
        end = jnp.where(source, source_range[1], plain_range[1])

        def one(n, carry):
            g = n // 4
            far = n // 8
            away = jnp.where(source, 2, 1) + 2 * far
            at = lax.rem(z + jnp.where(c == 0, ZS - away, away), ZS)
            h, k = order(lax.rem(n, 8))
            place = piece(at // 2, h, k)

            @pl.when(jnp.logical_or(jnp.logical_not(source), jnp.logical_or(far == 0, extra(g))))
            def _():
                wait(sbuf.at[place], z_recv.at[n])

                @pl.when(jnp.logical_or(far == 0, jnp.logical_and(jnp.logical_not(source), extra(g))))
                def _():
                    ring(place, n + jnp.where(source, 8, 0))

                share(place, p_recv.at[n])

            return carry

        lax.fori_loop(begin, end, one, 0)

    def product(m, h):
        def over(k, total):
            return total + jnp.dot(mboth[k], sbuf[piece(m, h, k)], preferred_element_type=F32)

        obuf[m * 2 + h] = lax.fori_loop(0, XS, over, jnp.zeros((2 * cols, half), F32))

        @pl.when(m != y)
        def _():
            put(obuf.at[m * 2 + h], orecv.at[y * 2 + h], o_send, o_recv.at[y, h], (XS * m + x, blk))

    def finish_own():
        @pl.when(source)
        def _():
            def one(h, carry):
                product(mine, h)
                return carry

            lax.fori_loop(0, 2, one, 0)

    def finish(g):
        def one(direction, carry):
            here = direction == c
            far = g // 2
            away = jnp.where(source, 2, 1) + 2 * far
            at = lax.rem(z + jnp.where(direction == 0, ZS - away, away), ZS)
            h = g % 2
            valid = jnp.logical_or(jnp.logical_not(source), far == 0)
            if far == 1:
                valid = jnp.logical_or(valid, g == 2 + direction)

            @pl.when(valid)
            def _():
                @pl.when(jnp.logical_not(here))
                def _():
                    for e in range(4):
                        place = piece(at // 2, h, lax.rem(2 * (1 - c) + e, 4))
                        wait(sbuf.at[place], p_recv.at[4 * g + e])

                product(at // 2, h)

            return carry

        lax.fori_loop(0, 2, one, 0)

    def spread(begin, end):
        for leaf in range(begin, end):
            for d in (1, 3, 2):
                put(mraw.at[x, leaf], mraw.at[x, leaf], m_send, m_recv.at[x], (XS * y + lax.rem(x + d, XS), blk))

    def gathered():
        for d in range(1, XS):
            other = lax.rem(x + d, XS)
            wait(weight.at[other], w_recv.at[other])
            wait(mraw.at[other], m_recv.at[other])

        def both(k, carry):
            w = weight[k]
            for leaf in range(leaves):
                row = jnp.concatenate([w[leaf : leaf + 1]] * (width // 128), axis=1)
                raw = mraw[k, leaf].astype(F32)
                span = slice(leaf * width, (leaf + 1) * width)
                mboth[k, :cols, span] = (raw * (1.0 - row)).astype(BF16)
                mboth[k, cols:, span] = (raw * row).astype(BF16)
            return carry

        lax.fori_loop(0, XS, both, 0)

    leaf_rhs = rhs_ref[...]
    leaf_solve = leaf_products(leaf_rhs, inv_ref, 1)
    rhs_terms = by_parent(leaf_products(leaf_solve, masked, 0))
    diag_rows = jnp.concatenate(
        [
            jnp.sum(masked[leaf].astype(F32) * solved[leaf].astype(F32), axis=0, keepdims=True)
            for leaf in range(leaves)
        ],
        axis=0,
    )
    opening = jnp.concatenate([rhs_terms, by_parent(diag_rows)], axis=0)
    pl.semaphore_wait(barrier, 2 * (ZS - 1) + (SCENS - 1) + XS)

    scen_send(first, opening, f_send, f_recv)

    to_x = 2 * lax.rem(z, 2) + c
    lane = x // 2
    itself = jnp.logical_and(to_x == x, lane == c)
    for h in range(2):
        place = piece(mine, h, x)
        slot = a_recv.at[h, lax.rem(x, 2)]

        @pl.when(itself)
        def _():
            pltpu.make_async_copy(own.at[h], sbuf.at[place], slot).start()

        @pl.when(jnp.logical_not(itself))
        def _():
            put(own.at[h], sbuf.at[place], a_send, slot, (XS * y + to_x, 2 * z + lane))

    for d in (1, 3, 2):
        put(weight.at[x], weight.at[x], w_send, w_recv.at[x], (XS * y + lax.rem(x + d, XS), blk))

    sums = collect(first, f_recv, SCENS)
    node_diag = ndiag_ref[...]
    reduced = nrhs_ref[...] - sums[0:2]
    scaling = node_diag + sums[2:4]
    state = reduced / scaling

    def sweep_a(it, value):
        blk_begin(it, leaf_products(of_parent(value), solved, 1))

    def sweep_b(it):
        inner = blk_collect(it)
        scen_send(u_at(it), by_parent(leaf_products(inner, masked, 0)), u_send, u_recv.at[it])

    def sweep_c(it, value):
        product_of = node_diag * value + collect(u_at(it), u_recv.at[it], SCENS)
        return value + DAMPING * (reduced - product_of) / scaling

    sweep_a(0, state)
    start_own(0)
    blk_send(0)
    start_other(0)
    sweep_b(0)
    spread(0, 2)
    start_own(1)
    start_other(1)
    state = sweep_c(0, state)
    sweep_a(1, state)
    serve((0, 2), (0, 0))
    blk_send(1)
    serve((2, 4), (0, 0))
    sweep_b(1)
    spread(2, 4)
    serve((4, 6), (0, 1))
    state = sweep_c(1, state)
    sweep_a(2, state)
    serve((6, 8), (1, 3))
    blk_send(2)
    serve((8, 8), (3, 5))
    sweep_b(2)
    gathered()
    finish_own()
    serve((8, 9), (5, 6))
    finish(0)
    state = sweep_c(2, state)
    sweep_a(3, state)
    serve((9, 11), (6, 8))
    blk_send(3)
    finish(1)
    serve((11, 12), (8, 9))
    sweep_b(3)
    serve((12, 13), (9, 11))
    state = sweep_c(3, state)
    node_ref[...] = state
    blk_begin(ITERS, leaf_products(of_parent(state), masked, 1))
    serve((13, 14), (11, 12))
    blk_send(ITERS)
    finish(2)
    serve((14, 16), (12, 16))
    finish(3)
    coupling = blk_collect(ITERS)
    leaf_ref[...] = leaf_products(leaf_rhs - coupling, inv_ref, 1)

    for h in range(2):
        total = obuf[y * 2 + h]
        for d in range(1, YS):
            other = lax.rem(y + d, YS)
            wait(orecv.at[other * 2 + h], o_recv.at[other, h])
            total = total + orecv[other * 2 + h]
        out_ref[0, :, h * half : (h + 1) * half] = total[:cols]
        out_ref[1, :, h * half : (h + 1) * half] = total[cols:]

    def drain(ref, count, sem):
        wait(ref.at[pl.ds(0, count)], sem)

    drain(first, SCENS - 1, f_send)
    drain(ubuf, ITERS * (SCENS - 1), u_send)
    drain(pair.at[:, 0], ITERS + 1, c_send)

    @pl.when(lax.rem(z + c, 2) == 1)
    def _():
        drain(tbuf, (ITERS + 1) * ZS, t_send)

    @pl.when(lax.rem(z + c, 2) == 0)
    def _():
        drain(tbuf, (ITERS + 1) * (ZS - 2), t_send)

    @pl.when(jnp.logical_not(itself))
    def _():
        drain(sbuf, 2, a_send)

    drain(weight, XS - 1, w_send)
    drain(mraw, XS - 1, m_send)

    @pl.when(source)
    def _():
        drain(sbuf, 16, z_send)
        drain(sbuf, 16, p_send)

    @pl.when(jnp.logical_not(source))
    def _():
        drain(sbuf, 12, z_send)
        drain(sbuf, 16, p_send)

    drain(obuf, 2 * (YS - 1), o_send)


def body(link, leaf_inverse, leaf_rhs, node_rhs, node_diag, parent, tile_mask):
    leaves, width, cols = link.shape
    nodes = node_rhs.shape[0]
    vmem = pl.BlockSpec(memory_space=pltpu.VMEM)
    smem = pl.BlockSpec(memory_space=pltpu.SMEM)
    dma = pltpu.SemaphoreType.DMA
    half = cols // 2
    return pl.pallas_call(
        step_kernel,
        out_shape=(
            jax.ShapeDtypeStruct((nodes, cols), F32),
            jax.ShapeDtypeStruct((leaves, width), F32),
            jax.ShapeDtypeStruct((nodes, cols, cols), F32),
        ),
        in_specs=[smem, smem] + [vmem] * 5,
        out_specs=(vmem,) * 3,
        scratch_shapes=[
            pltpu.VMEM((leaves, width, cols), BF16),
            pltpu.VMEM((leaves, width, cols), BF16),
            pltpu.VMEM((SCENS, 2 * nodes, cols), F32),
            pltpu.VMEM((ITERS * SCENS, nodes, cols), F32),
            pltpu.VMEM(((ITERS + 1) * ZS, leaves, width), F32),
            pltpu.VMEM((ITERS + 1, 2, leaves, width), F32),
            pltpu.VMEM((2, leaves * width, half), BF16),
            pltpu.VMEM((2 * YS * XS, leaves * width, half), BF16),
            pltpu.VMEM((XS, leaves, cols, width), BF16),
            pltpu.VMEM((XS, 8, 128), F32),
            pltpu.VMEM((XS, nodes * cols, leaves * width), BF16),
            pltpu.VMEM((2 * YS, nodes * cols, half), F32),
            pltpu.VMEM((2 * YS, nodes * cols, half), F32),
            dma, dma, dma, dma((ITERS,)), dma, dma((ITERS + 1,)), dma, dma((ITERS + 1,)),
            dma, dma((2, 2)), dma, dma((XS,)), dma, dma((XS,)), dma, dma((16,)),
            dma, dma((16,)), dma((2, 2)), dma, dma((YS, 2)),
        ],
        compiler_params=pltpu.CompilerParams(collective_id=0, has_side_effects=True, vmem_limit_bytes=60000 * 1024),
        name="step",
    )(parent, tile_mask.reshape(-1), link, leaf_inverse, leaf_rhs, node_rhs, node_diag)


def solution(mesh):
    in_specs = (
        P("scen", None, "blk"),
        P("scen", None, None),
        P("scen", None),
        P(None, "blk"),
        P(None, "blk"),
        P("scen"),
        P("scen", "blk"),
    )
    out_specs = (P(None, "blk"), P("scen", None), P(None, "blk", "scen"))
    return jax.shard_map(body, mesh=mesh, in_specs=in_specs, out_specs=out_specs, check_vma=False)
```

```python
import jax
import jax.numpy as jnp
from jax import lax
from jax.experimental import pallas as pl
from jax.experimental.pallas import tpu as pltpu
from jax.sharding import PartitionSpec as P

ITERS = 4
DAMPING = 0.4
MESH = pl.DeviceIdType.MESH
F32 = jnp.float32
BF16 = jnp.bfloat16
XS = 4
YS = 4
ZS = 8
SCENS = XS * YS


def split_rows(v):
    hi = v.astype(BF16).astype(F32)
    rest = v - hi
    mid = rest.astype(BF16).astype(F32)
    low = rest - mid
    return jnp.concatenate([hi, mid, low, jnp.zeros_like(v)], axis=0).astype(BF16)


def leaf_products(v, mats_ref, contract):
    parts = split_rows(v)
    leaves = mats_ref.shape[0]
    row = lax.broadcasted_iota(jnp.int32, v.shape, 0)
    total = jnp.zeros(v.shape, F32)
    for leaf in range(leaves):
        out = lax.dot_general(
            parts, mats_ref[leaf], (((1,), (contract,)), ((), ())), preferred_element_type=F32
        )
        out = out[0:4] + out[4:8] + out[8:12]
        total = total + jnp.where(row == leaf, out, 0.0)
    return total


def step_kernel(
    parent_ref, mask_ref, link_ref, inv_ref, rhs_ref, nrhs_ref, ndiag_ref,
    node_ref, leaf_ref, out_ref,
    masked, solved, first, ubuf, tbuf, pair,
    own, sbuf, mraw, weight, mboth, obuf, orecv,
    f_send, f_recv, u_send, u_recv, t_send, t_recv, c_send, c_recv,
    a_send, a_recv, m_send, m_recv, w_send, w_recv, z_send, z_recv,
    p_send, p_recv, q_recv, o_send, o_recv, narrow, n_send, n_recv,
):
    scen = lax.axis_index("scen")
    blk = lax.axis_index("blk")
    y, x = scen // XS, lax.rem(scen, XS)
    z, c = blk // 2, lax.rem(blk, 2)
    leaves, width, cols = link_ref.shape
    half = cols // 2
    source = lax.rem(z, 2) == x // 2
    partner = (scen, 2 * z + 1 - c)
    barrier = pltpu.get_barrier_semaphore()

    def greet(s, b):
        pl.semaphore_signal(barrier, inc=1, device_id=(s, b), device_id_type=MESH)

    for d in range(1, ZS):
        for e in range(2):
            greet(scen, 2 * lax.rem(z + d, ZS) + e)
    for d in range(1, SCENS):
        greet(lax.rem(scen + d, SCENS), blk)
    for d in range(XS):
        greet(XS * y + lax.rem(x + d, XS), 2 * z + 1 - c)

    def put(src, dst, send, recv, target):
        pltpu.make_async_remote_copy(
            src_ref=src, dst_ref=dst, send_sem=send, recv_sem=recv, device_id=target, device_id_type=MESH
        ).start()

    def wait(ref, sem):
        pltpu.make_async_copy(ref, ref, sem).wait()

    for leaf in range(leaves):
        m = link_ref[leaf] * mask_ref[leaf].astype(BF16)
        s = jnp.dot(inv_ref[leaf], m, preferred_element_type=F32).astype(BF16)
        masked[leaf] = m
        solved[leaf] = s
        for h in range(2):
            own[h, leaf * width : (leaf + 1) * width, :] = s[:, h * half : (h + 1) * half]
    owner = [parent_ref[leaf].astype(F32) for leaf in range(leaves)]
    weight[x] = jnp.concatenate(
        [jnp.full((1, 128), owner[leaf], F32) for leaf in range(leaves)] + [jnp.zeros((8 - leaves, 128), F32)],
        axis=0,
    )

    row2 = lax.broadcasted_iota(jnp.int32, nrhs_ref.shape, 0)
    row4 = lax.broadcasted_iota(jnp.int32, rhs_ref.shape, 0)

    def by_parent(rows):
        total = jnp.zeros(nrhs_ref.shape, F32)
        for leaf in range(leaves):
            share_of = jnp.where(row2 == 0, 1.0 - owner[leaf], owner[leaf])
            total = total + share_of * rows[leaf : leaf + 1]
        return total

    def of_parent(values):
        total = jnp.zeros(rhs_ref.shape, F32)
        for leaf in range(leaves):
            mine = values[0:1] * (1.0 - owner[leaf]) + values[1:2] * owner[leaf]
            total = total + jnp.where(row4 == leaf, mine, 0.0)
        return total

    def scen_send(buf, value, send, recv):
        buf[scen] = value
        for d in range(1, SCENS):
            put(buf.at[scen], buf.at[scen], send, recv, (lax.rem(scen + d, SCENS), blk))

    def collect(buf, recv, count):
        wait(buf.at[pl.ds(0, count - 1)], recv)
        total = buf[0]
        for j in range(1, count):
            total = total + buf[j]
        return total

    def blk_begin(it, value):
        pair[it, c] = value
        put(pair.at[it, c], pair.at[it, c], c_send, c_recv.at[it], partner)

    def blk_send(it):
        wait(pair.at[it, 0], c_recv.at[it])
        at = ZS * it + z
        tbuf[at] = pair[it, 0] + pair[it, 1]
        for d in range(1, ZS // 2 + 1):
            to = lax.rem(z + jnp.where(c == 0, ZS - d, d), ZS)

            def both_cores():
                for e in range(2):
                    put(tbuf.at[at], tbuf.at[at], t_send, t_recv.at[it], (scen, 2 * to + e))

            if d < ZS // 2:
                both_cores()
            else:
                pl.when(lax.rem(z + c, 2) == 1)(both_cores)

    def blk_collect(it):
        return collect(tbuf.at[pl.ds(ZS * it, ZS)], t_recv.at[it], ZS)

    def u_at(it):
        return ubuf.at[pl.ds(SCENS * it, SCENS)]

    def piece(m, h, k):
        return (m * 2 + h) * XS + k

    def ring(place, step):
        to = lax.rem(z + jnp.where(c == 0, 1, ZS - 1), ZS)
        put(sbuf.at[place], sbuf.at[place], z_send, z_recv.at[step], (scen, 2 * to + c))

    def share(place, slot):
        put(sbuf.at[place], sbuf.at[place], p_send, slot, partner)

    mine = z // 2

    beside = x + 1 - 2 * lax.rem(x, 2)

    def order(q):
        h = jnp.where(jnp.logical_or(q == 1, q >= 5), 1, 0)
        j = jnp.where(q < 2, 0, jnp.where(q < 5, q - 1, q - 4))
        k = jnp.where(j == 0, x, jnp.where(j == 1, beside, lax.rem(jnp.where(j == 2, beside, x) + 2, XS)))
        return h, k

    def far_order(way, p):
        return jnp.where(way == 0, p, jnp.where(p < 2, p, jnp.where(p < 6, p + 2, p - 4)))

    def crosses(way, p):
        return jnp.logical_and(p >= 2 * way, p < 4 + 2 * way)

    def start_own(begin, end):
        @pl.when(source)
        def _():
            for q in range(begin, end):
                h, k = order(q)
                place = piece(mine, h, k)
                direct = k // 2 == c

                @pl.when(direct)
                def _():
                    wait(sbuf.at[place], a_recv.at[h, lax.rem(k, 2)])
                    ring(place, q)
                    share(place, q_recv.at[h, lax.rem(k, 2)])

                @pl.when(jnp.logical_not(direct))
                def _():
                    wait(sbuf.at[place], q_recv.at[h, lax.rem(k, 2)])
                    ring(place, q)

    def arrival(way, n):
        far = n // 8
        p = lax.rem(n, 8)
        away = jnp.where(source, 2, 1) + 2 * far
        at = lax.rem(z + jnp.where(way == 0, ZS - away, away), ZS)
        h, k = order(jnp.where(far == 0, p, far_order(way, p)))
        comes = jnp.logical_or(jnp.logical_not(source), jnp.logical_or(far == 0, crosses(way, p)))
        return piece(at // 2, h, k), at // 2, comes

    def serve(plain_range, source_range):
        begin = jnp.where(source, source_range[0], plain_range[0])
        end = jnp.where(source, source_range[1], plain_range[1])

        def one(n, carry):
            place, at, comes = arrival(c, n)
            far = n // 8
            p = lax.rem(n, 8)

            @pl.when(comes)
            def _():
                wait(sbuf.at[place], z_recv.at[n])

                @pl.when(jnp.logical_and(jnp.logical_not(source), jnp.logical_or(far == 0, crosses(c, p))))
                def _():
                    ring(place, n)

                @pl.when(jnp.logical_and(source, far == 0))
                def _():
                    @pl.when(jnp.logical_or(c == 0, p < 2))
                    def _():
                        ring(place, n + 8)

                    @pl.when(jnp.logical_and(c == 1, p >= 4))
                    def _():
                        ring(place, n + 6)

                    @pl.when(jnp.logical_and(c == 1, p == 7))
                    def _():
                        for q in (2, 3):
                            ring(piece(at, *order(q)), 12 + q)

                share(place, p_recv.at[n])

            return carry

        lax.fori_loop(begin, end, one, 0)

    def shared(plain_range, source_range):
        begin = jnp.where(source, source_range[0], plain_range[0])
        end = jnp.where(source, source_range[1], plain_range[1])

        def one(n, carry):
            place, at, comes = arrival(1 - c, n)

            @pl.when(comes)
            def _():
                wait(sbuf.at[place], p_recv.at[n])

            return carry

        lax.fori_loop(begin, end, one, 0)

    def product(m, halves):
        def over(k, carry):
            right = [sbuf[piece(m, h, k)] for h in halves]
            right = right[0] if len(right) == 1 else jnp.concatenate(right, axis=1)
            out = jnp.dot(mboth[k], right, preferred_element_type=F32)
            for i, h in enumerate(halves):
                part = out[:, i * half : (i + 1) * half]
                obuf[m * 2 + h] = jnp.where(k == 0, part, obuf[m * 2 + h] + part)
            return carry

        lax.fori_loop(0, XS, over, 0)

    across = lax.rem(y + 2, YS)

    def ship(m, halves):
        @pl.when(jnp.logical_and(m != y, m != across))
        def _():
            for h in halves:
                put(obuf.at[m * 2 + h], orecv.at[y * 2 + h], o_send, o_recv.at[y], (XS * m + x, blk))

        @pl.when(m == across)
        def _():
            for h in halves:
                narrow[h] = obuf[m * 2 + h].astype(BF16)
                put(narrow.at[h], narrow.at[2 + h], n_send, n_recv, (XS * m + x, blk))

    def leaves_by(m):
        away = lax.rem(m - y + YS, YS)
        up = jnp.logical_or(away == 1, jnp.logical_and(away == 2, lax.rem(y, 2) == 0))
        return jnp.where(away == 0, 0, jnp.where(up, 1, 2))

    def near(way):
        away = jnp.where(source, 2, 1)
        return lax.rem(z + (ZS - away if way == 0 else away), ZS) // 2

    def free_for(way):
        link = leaves_by(near(way))
        taken = jnp.logical_and(source, link == leaves_by(mine))
        if way == 1:
            taken = jnp.logical_or(taken, link == leaves_by(near(0)))
        return jnp.logical_not(taken)

    def ship_early(way):
        @pl.when(free_for(way))
        def _():
            ship(near(way), (0,))

    def ship_own_late():
        @pl.when(source)
        def _():
            ship(mine, (1,))

    def ship_late(way):
        @pl.when(jnp.logical_not(free_for(way)))
        def _():
            ship(near(way), (0,))

        ship(near(way), (1,))

    def finish_own():
        @pl.when(source)
        def _():
            product(mine, (0, 1))
            ship(mine, (0,))

    def finish_far(i):
        def one(way, carry):
            at = lax.rem(z + jnp.where(way == 0, ZS - 3, 3), ZS)

            def with_half(h):
                @pl.when(way == (i + h) % 2)
                def _():
                    product(at // 2, (h,))
                    ship(at // 2, (h,))

            @pl.when(jnp.logical_not(source))
            def _():
                for h in range(2):
                    with_half(h)

            return carry

        lax.fori_loop(0, 2, one, 0)

    def finish_farthest():
        @pl.when(source)
        def _():
            product(lax.rem(z + 4, ZS) // 2, (0, 1))
            ship(lax.rem(z + 4, ZS) // 2, (0, 1))

    def spread(begin, end):
        for leaf in range(begin, end):
            for d in (1, 3, 2):
                put(mraw.at[x, leaf], mraw.at[x, leaf], m_send, m_recv.at[x], (XS * y + lax.rem(x + d, XS), blk))

    def turn():
        for leaf in range(leaves):
            mraw[x, leaf] = masked[leaf].astype(F32).T.astype(BF16)

    def gathered():
        for d in range(1, XS):
            other = lax.rem(x + d, XS)
            wait(weight.at[other], w_recv.at[other])
            wait(mraw.at[other], m_recv.at[other])

        def both(k, carry):
            w = weight[k]
            for leaf in range(leaves):
                row = jnp.concatenate([w[leaf : leaf + 1]] * (width // 128), axis=1).astype(BF16)
                raw = mraw[k, leaf]
                span = slice(leaf * width, (leaf + 1) * width)
                mboth[k, :cols, span] = raw * (1 - row)
                mboth[k, cols:, span] = raw * row
            return carry

        lax.fori_loop(0, XS, both, 0)

    leaf_rhs = rhs_ref[...]
    leaf_solve = leaf_products(leaf_rhs, inv_ref, 1)
    rhs_terms = by_parent(leaf_products(leaf_solve, masked, 0))
    diag_rows = jnp.concatenate(
        [
            jnp.sum(masked[leaf].astype(F32) * solved[leaf].astype(F32), axis=0, keepdims=True)
            for leaf in range(leaves)
        ],
        axis=0,
    )
    opening = jnp.concatenate([rhs_terms, by_parent(diag_rows)], axis=0)
    pl.semaphore_wait(barrier, 2 * (ZS - 1) + (SCENS - 1) + XS)

    scen_send(first, opening, f_send, f_recv)

    to_x = 2 * lax.rem(z, 2) + c
    lane = x // 2
    itself = jnp.logical_and(to_x == x, lane == c)
    for h in range(2):
        place = piece(mine, h, x)
        slot = a_recv.at[h, lax.rem(x, 2)]

        @pl.when(itself)
        def _():
            pltpu.make_async_copy(own.at[h], sbuf.at[place], slot).start()

        @pl.when(jnp.logical_not(itself))
        def _():
            put(own.at[h], sbuf.at[place], a_send, slot, (XS * y + to_x, 2 * z + lane))

    for d in (1, 3, 2):
        put(weight.at[x], weight.at[x], w_send, w_recv.at[x], (XS * y + lax.rem(x + d, XS), blk))

    start_own(0, 2)
    sums = collect(first, f_recv, SCENS)
    node_diag = ndiag_ref[...]
    reduced = nrhs_ref[...] - sums[0:2]
    scaling = node_diag + sums[2:4]
    state = reduced / scaling

    def sweep_a(it, value):
        blk_begin(it, leaf_products(of_parent(value), solved, 1))

    def sweep_b(it):
        inner = blk_collect(it)
        scen_send(u_at(it), by_parent(leaf_products(inner, masked, 0)), u_send, u_recv.at[it])

    def sweep_c(it, value):
        product_of = node_diag * value + collect(u_at(it), u_recv.at[it], SCENS)
        return value + DAMPING * (reduced - product_of) / scaling

    sweep_a(0, state)
    turn()
    blk_send(0)
    start_own(2, 5)
    sweep_b(0)
    spread(0, 2)
    start_own(5, 8)
    serve((0, 2), (0, 0))
    state = sweep_c(0, state)
    sweep_a(1, state)
    serve((2, 4), (0, 0))
    blk_send(1)
    serve((4, 5), (0, 0))
    sweep_b(1)
    spread(2, 4)
    serve((5, 7), (0, 2))
    state = sweep_c(1, state)
    sweep_a(2, state)
    serve((7, 8), (2, 5))
    blk_send(2)
    serve((8, 9), (5, 6))
    sweep_b(2)
    gathered()
    finish_own()
    serve((9, 11), (6, 8))
    shared((0, 8), (0, 8))
    product(near(0), (0, 1))
    state = sweep_c(2, state)
    sweep_a(3, state)
    serve((11, 12), (8, 8))
    blk_send(3)
    product(near(1), (0, 1))
    serve((12, 13), (8, 9))
    sweep_b(3)
    ship_own_late()
    ship(near(0), (0, 1))
    ship(near(1), (0, 1))
    serve((13, 14), (9, 14))
    shared((8, 14), (8, 14))
    finish_far(0)
    finish_farthest()
    state = sweep_c(3, state)
    node_ref[...] = state
    blk_begin(ITERS, leaf_products(of_parent(state), masked, 1))
    serve((14, 16), (14, 16))
    blk_send(ITERS)
    shared((14, 16), (14, 16))
    finish_far(1)
    coupling = blk_collect(ITERS)
    leaf_ref[...] = leaf_products(leaf_rhs - coupling, inv_ref, 1)

    for d in (1, YS - 1):
        other = lax.rem(y + d, YS)
        wait(orecv.at[pl.ds(2 * other, 2)], o_recv.at[other])
    wait(narrow.at[pl.ds(2, 2)], n_recv)
    for h in range(2):
        total = obuf[y * 2 + h]
        for d in (1, YS - 1):
            total = total + orecv[lax.rem(y + d, YS) * 2 + h]
        total = total + narrow[2 + h].astype(F32)
        out_ref[0, :, h * half : (h + 1) * half] = total[:cols]
        out_ref[1, :, h * half : (h + 1) * half] = total[cols:]

    def drain(ref, count, sem):
        wait(ref.at[pl.ds(0, count)], sem)

    drain(first, SCENS - 1, f_send)
    drain(ubuf, ITERS * (SCENS - 1), u_send)
    drain(pair.at[:, 0], ITERS + 1, c_send)

    @pl.when(lax.rem(z + c, 2) == 1)
    def _():
        drain(tbuf, (ITERS + 1) * ZS, t_send)

    @pl.when(lax.rem(z + c, 2) == 0)
    def _():
        drain(tbuf, (ITERS + 1) * (ZS - 2), t_send)

    @pl.when(jnp.logical_not(itself))
    def _():
        drain(sbuf, 2, a_send)

    drain(weight, XS - 1, w_send)
    drain(mraw, XS - 1, m_send)

    @pl.when(source)
    def _():
        drain(sbuf, 16, z_send)
        drain(sbuf, 16, p_send)

    @pl.when(jnp.logical_not(source))
    def _():
        drain(sbuf, 12, z_send)
        drain(sbuf, 16, p_send)

    drain(obuf, 2 * (YS - 2), o_send)
    drain(narrow, 2, n_send)


def body(link, leaf_inverse, leaf_rhs, node_rhs, node_diag, parent, tile_mask):
    leaves, width, cols = link.shape
    nodes = node_rhs.shape[0]
    vmem = pl.BlockSpec(memory_space=pltpu.VMEM)
    smem = pl.BlockSpec(memory_space=pltpu.SMEM)
    dma = pltpu.SemaphoreType.DMA
    half = cols // 2
    return pl.pallas_call(
        step_kernel,
        out_shape=(
            jax.ShapeDtypeStruct((nodes, cols), F32),
            jax.ShapeDtypeStruct((leaves, width), F32),
            jax.ShapeDtypeStruct((nodes, cols, cols), F32),
        ),
        in_specs=[smem, smem] + [vmem] * 5,
        out_specs=(vmem,) * 3,
        scratch_shapes=[
            pltpu.VMEM((leaves, width, cols), BF16),
            pltpu.VMEM((leaves, width, cols), BF16),
            pltpu.VMEM((SCENS, 2 * nodes, cols), F32),
            pltpu.VMEM((ITERS * SCENS, nodes, cols), F32),
            pltpu.VMEM(((ITERS + 1) * ZS, leaves, width), F32),
            pltpu.VMEM((ITERS + 1, 2, leaves, width), F32),
            pltpu.VMEM((2, leaves * width, half), BF16),
            pltpu.VMEM((2 * YS * XS, leaves * width, half), BF16),
            pltpu.VMEM((XS, leaves, cols, width), BF16),
            pltpu.VMEM((XS, 8, 128), F32),
            pltpu.VMEM((XS, nodes * cols, leaves * width), BF16),
            pltpu.VMEM((2 * YS, nodes * cols, half), F32),
            pltpu.VMEM((2 * YS, nodes * cols, half), F32),
            dma, dma, dma, dma((ITERS,)), dma, dma((ITERS + 1,)), dma, dma((ITERS + 1,)),
            dma, dma((2, 2)), dma, dma((XS,)), dma, dma((XS,)), dma, dma((16,)),
            dma, dma((16,)), dma((2, 2)), dma, dma((YS,)),
            pltpu.VMEM((4, nodes * cols, half), BF16), dma, dma,
        ],
        compiler_params=pltpu.CompilerParams(collective_id=0, has_side_effects=True, vmem_limit_bytes=60000 * 1024),
        name="step",
    )(parent, tile_mask.reshape(-1), link, leaf_inverse, leaf_rhs, node_rhs, node_diag)


def solution(mesh):
    in_specs = (
        P("scen", None, "blk"),
        P("scen", None, None),
        P("scen", None),
        P(None, "blk"),
        P(None, "blk"),
        P("scen"),
        P("scen", "blk"),
    )
    out_specs = (P(None, "blk"), P("scen", None), P(None, "blk", "scen"))
    return jax.shard_map(body, mesh=mesh, in_specs=in_specs, out_specs=out_specs, check_vma=False)
```

```python
import jax
import jax.numpy as jnp
from jax import lax
from jax.experimental import pallas as pl
from jax.experimental.pallas import tpu as pltpu
from jax.sharding import PartitionSpec as P

ITERS = 4
DAMPING = 0.4
MESH = pl.DeviceIdType.MESH
F32 = jnp.float32
BF16 = jnp.bfloat16
XS = 4
YS = 4
ZS = 8
SCENS = XS * YS


def split_rows(v):
    hi = v.astype(BF16).astype(F32)
    rest = v - hi
    mid = rest.astype(BF16).astype(F32)
    low = rest - mid
    return jnp.concatenate([hi, mid, low, jnp.zeros_like(v)], axis=0).astype(BF16)


def leaf_products(v, mats_ref, contract):
    parts = split_rows(v)
    leaves = mats_ref.shape[0]
    row = lax.broadcasted_iota(jnp.int32, v.shape, 0)
    total = jnp.zeros(v.shape, F32)
    for leaf in range(leaves):
        out = lax.dot_general(
            parts, mats_ref[leaf], (((1,), (contract,)), ((), ())), preferred_element_type=F32
        )
        out = out[0:4] + out[4:8] + out[8:12]
        total = total + jnp.where(row == leaf, out, 0.0)
    return total


def step_kernel(
    parent_ref, mask_ref, link_in, inv_in, rhs_ref, nrhs_ref, ndiag_ref,
    node_ref, leaf_ref, out_ref,
    masked, solved, first, ubuf, tbuf, pair,
    own, sbuf, mraw, weight, mboth, obuf, orecv,
    f_send, f_recv, u_send, u_recv, t_send, t_recv, c_send, c_recv,
    a_send, a_recv, m_send, m_recv, w_send, w_recv, z_send, z_recv,
    p_send, p_recv, q_recv, o_send, o_recv, narrow, n_send, n_recv, link_ref, inv_ref, in_sem,
):
    fetch_inv = pltpu.make_async_copy(inv_in, inv_ref, in_sem.at[0])
    fetch_inv.start()
    fetch_link = pltpu.make_async_copy(link_in, link_ref, in_sem.at[1])
    fetch_link.start()
    scen = lax.axis_index("scen")
    blk = lax.axis_index("blk")
    y, x = scen // XS, lax.rem(scen, XS)
    z, c = blk // 2, lax.rem(blk, 2)
    leaves, width, cols = link_ref.shape
    half = cols // 2
    source = lax.rem(z, 2) == x // 2
    partner = (scen, 2 * z + 1 - c)
    barrier = pltpu.get_barrier_semaphore()

    def greet(s, b):
        pl.semaphore_signal(barrier, inc=1, device_id=(s, b), device_id_type=MESH)

    for d in range(1, ZS):
        for e in range(2):
            greet(scen, 2 * lax.rem(z + d, ZS) + e)
    for d in range(1, SCENS):
        greet(lax.rem(scen + d, SCENS), blk)
    for d in range(XS):
        greet(XS * y + lax.rem(x + d, XS), 2 * z + 1 - c)

    def put(src, dst, send, recv, target):
        pltpu.make_async_remote_copy(
            src_ref=src, dst_ref=dst, send_sem=send, recv_sem=recv, device_id=target, device_id_type=MESH
        ).start()

    def wait(ref, sem):
        pltpu.make_async_copy(ref, ref, sem).wait()

    fetch_inv.wait()
    fetch_link.wait()
    for leaf in range(leaves):
        m = link_ref[leaf] * mask_ref[leaf].astype(BF16)
        s = jnp.dot(inv_ref[leaf], m, preferred_element_type=F32).astype(BF16)
        masked[leaf] = m
        solved[leaf] = s
        for h in range(2):
            own[h, leaf * width : (leaf + 1) * width, :] = s[:, h * half : (h + 1) * half]
    owner = [parent_ref[leaf].astype(F32) for leaf in range(leaves)]
    weight[x] = jnp.concatenate(
        [jnp.full((1, 128), owner[leaf], F32) for leaf in range(leaves)] + [jnp.zeros((8 - leaves, 128), F32)],
        axis=0,
    )

    row2 = lax.broadcasted_iota(jnp.int32, nrhs_ref.shape, 0)
    row4 = lax.broadcasted_iota(jnp.int32, rhs_ref.shape, 0)

    def by_parent(rows):
        total = jnp.zeros(nrhs_ref.shape, F32)
        for leaf in range(leaves):
            share_of = jnp.where(row2 == 0, 1.0 - owner[leaf], owner[leaf])
            total = total + share_of * rows[leaf : leaf + 1]
        return total

    def of_parent(values):
        total = jnp.zeros(rhs_ref.shape, F32)
        for leaf in range(leaves):
            mine = values[0:1] * (1.0 - owner[leaf]) + values[1:2] * owner[leaf]
            total = total + jnp.where(row4 == leaf, mine, 0.0)
        return total

    def scen_send(buf, value, send, recv):
        buf[scen] = value
        for d in range(1, SCENS):
            put(buf.at[scen], buf.at[scen], send, recv, (lax.rem(scen + d, SCENS), blk))

    def collect(buf, recv, count):
        wait(buf.at[pl.ds(0, count - 1)], recv)
        total = buf[0]
        for j in range(1, count):
            total = total + buf[j]
        return total

    def blk_begin(it, value):
        pair[it, c] = value
        put(pair.at[it, c], pair.at[it, c], c_send, c_recv.at[it], partner)

    def blk_send(it):
        wait(pair.at[it, 0], c_recv.at[it])
        at = ZS * it + z
        tbuf[at] = pair[it, 0] + pair[it, 1]
        for d in range(1, ZS // 2 + 1):
            to = lax.rem(z + jnp.where(c == 0, ZS - d, d), ZS)

            def both_cores():
                for e in range(2):
                    put(tbuf.at[at], tbuf.at[at], t_send, t_recv.at[it], (scen, 2 * to + e))

            if d < ZS // 2:
                both_cores()
            else:
                pl.when(lax.rem(z + c, 2) == 1)(both_cores)

    def blk_collect(it):
        return collect(tbuf.at[pl.ds(ZS * it, ZS)], t_recv.at[it], ZS)

    def u_at(it):
        return ubuf.at[pl.ds(SCENS * it, SCENS)]

    def piece(m, h, k):
        return (m * 2 + h) * XS + k

    def ring(place, step):
        to = lax.rem(z + jnp.where(c == 0, 1, ZS - 1), ZS)
        put(sbuf.at[place], sbuf.at[place], z_send, z_recv.at[step], (scen, 2 * to + c))

    def share(place, slot):
        put(sbuf.at[place], sbuf.at[place], p_send, slot, partner)

    mine = z // 2

    beside = x + 1 - 2 * lax.rem(x, 2)

    def order(q):
        h = jnp.where(jnp.logical_or(q == 1, q >= 5), 1, 0)
        j = jnp.where(q < 2, 0, jnp.where(q < 5, q - 1, q - 4))
        k = jnp.where(j == 0, x, jnp.where(j == 1, beside, lax.rem(jnp.where(j == 2, beside, x) + 2, XS)))
        return h, k

    def far_order(way, p):
        return jnp.where(way == 0, p, jnp.where(p < 2, p, jnp.where(p < 6, p + 2, p - 4)))

    def crosses(way, p):
        return jnp.logical_and(p >= 2 * way, p < 4 + 2 * way)

    def start_own(begin, end):
        @pl.when(source)
        def _():
            for q in range(begin, end):
                h, k = order(q)
                place = piece(mine, h, k)
                direct = k // 2 == c

                @pl.when(direct)
                def _():
                    wait(sbuf.at[place], a_recv.at[h, lax.rem(k, 2)])
                    ring(place, q)
                    share(place, q_recv.at[h, lax.rem(k, 2)])

                @pl.when(jnp.logical_not(direct))
                def _():
                    wait(sbuf.at[place], q_recv.at[h, lax.rem(k, 2)])
                    ring(place, q)

    def arrival(way, n):
        far = n // 8
        p = lax.rem(n, 8)
        away = jnp.where(source, 2, 1) + 2 * far
        at = lax.rem(z + jnp.where(way == 0, ZS - away, away), ZS)
        h, k = order(jnp.where(far == 0, p, far_order(way, p)))
        comes = jnp.logical_or(jnp.logical_not(source), jnp.logical_or(far == 0, crosses(way, p)))
        return piece(at // 2, h, k), at // 2, comes

    def serve(plain_range, source_range):
        begin = jnp.where(source, source_range[0], plain_range[0])
        end = jnp.where(source, source_range[1], plain_range[1])

        def one(n, carry):
            place, at, comes = arrival(c, n)
            far = n // 8
            p = lax.rem(n, 8)

            @pl.when(comes)
            def _():
                wait(sbuf.at[place], z_recv.at[n])

                @pl.when(jnp.logical_and(jnp.logical_not(source), jnp.logical_or(far == 0, crosses(c, p))))
                def _():
                    ring(place, n)

                @pl.when(jnp.logical_and(source, far == 0))
                def _():
                    @pl.when(jnp.logical_or(c == 0, p < 2))
                    def _():
                        ring(place, n + 8)

                    @pl.when(jnp.logical_and(c == 1, p >= 4))
                    def _():
                        ring(place, n + 6)

                    @pl.when(jnp.logical_and(c == 1, p == 7))
                    def _():
                        for q in (2, 3):
                            ring(piece(at, *order(q)), 12 + q)

                share(place, p_recv.at[n])

            return carry

        lax.fori_loop(begin, end, one, 0)

    def shared(plain_range, source_range):
        begin = jnp.where(source, source_range[0], plain_range[0])
        end = jnp.where(source, source_range[1], plain_range[1])

        def one(n, carry):
            place, at, comes = arrival(1 - c, n)

            @pl.when(comes)
            def _():
                wait(sbuf.at[place], p_recv.at[n])

            return carry

        lax.fori_loop(begin, end, one, 0)

    def product(m, halves):
        def over(k, carry):
            right = [sbuf[piece(m, h, k)] for h in halves]
            right = right[0] if len(right) == 1 else jnp.concatenate(right, axis=1)
            out = jnp.dot(mboth[k], right, preferred_element_type=F32)
            for i, h in enumerate(halves):
                part = out[:, i * half : (i + 1) * half]
                obuf[m * 2 + h] = jnp.where(k == 0, part, obuf[m * 2 + h] + part)
            return carry

        lax.fori_loop(0, XS, over, 0)

    across = lax.rem(y + 2, YS)

    def ship(m, halves):
        @pl.when(jnp.logical_and(m != y, m != across))
        def _():
            for h in halves:
                put(obuf.at[m * 2 + h], orecv.at[y * 2 + h], o_send, o_recv.at[y], (XS * m + x, blk))

        @pl.when(m == across)
        def _():
            for h in halves:
                narrow[h] = obuf[m * 2 + h].astype(BF16)
                put(narrow.at[h], narrow.at[2 + h], n_send, n_recv, (XS * m + x, blk))

    def leaves_by(m):
        away = lax.rem(m - y + YS, YS)
        up = jnp.logical_or(away == 1, jnp.logical_and(away == 2, lax.rem(y, 2) == 0))
        return jnp.where(away == 0, 0, jnp.where(up, 1, 2))

    def near(way):
        away = jnp.where(source, 2, 1)
        return lax.rem(z + (ZS - away if way == 0 else away), ZS) // 2

    def free_for(way):
        link = leaves_by(near(way))
        taken = jnp.logical_and(source, link == leaves_by(mine))
        if way == 1:
            taken = jnp.logical_or(taken, link == leaves_by(near(0)))
        return jnp.logical_not(taken)

    def ship_early(way, at_source=True):
        @pl.when(jnp.logical_and(free_for(way), jnp.logical_or(at_source, jnp.logical_not(source))))
        def _():
            ship(near(way), (0,))

    def ship_own_late():
        @pl.when(source)
        def _():
            ship(mine, (1,))

    def ship_late(way, at_source=True):
        @pl.when(jnp.logical_not(jnp.logical_and(free_for(way), jnp.logical_or(at_source, jnp.logical_not(source)))))
        def _():
            ship(near(way), (0,))

        ship(near(way), (1,))

    def finish_own():
        @pl.when(source)
        def _():
            product(mine, (0, 1))
            ship(mine, (0,))

    def far_halves(i, act):
        def one(way, carry):
            m = lax.rem(z + jnp.where(way == 0, ZS - 3, 3), ZS) // 2

            @pl.when(jnp.logical_not(source))
            def _():
                for h in range(2):
                    @pl.when(way == (i + h) % 2)
                    def _():
                        act(m, (h,))

            return carry

        lax.fori_loop(0, 2, one, 0)

        @pl.when(source)
        def _():
            act(lax.rem(z + 4, ZS) // 2, (i,))

    def both_acts(m, halves):
        product(m, halves)
        ship(m, halves)

    def spread(begin, end):
        for leaf in range(begin, end):
            for d in (1, 3, 2):
                put(mraw.at[x, leaf], mraw.at[x, leaf], m_send, m_recv.at[x], (XS * y + lax.rem(x + d, XS), blk))

    def turn():
        for leaf in range(leaves):
            mraw[x, leaf] = masked[leaf].astype(F32).T.astype(BF16)

    def gathered():
        for d in range(1, XS):
            other = lax.rem(x + d, XS)
            wait(weight.at[other], w_recv.at[other])
            wait(mraw.at[other], m_recv.at[other])

        def both(k, carry):
            w = weight[k]
            for leaf in range(leaves):
                row = jnp.concatenate([w[leaf : leaf + 1]] * (width // 128), axis=1).astype(BF16)
                raw = mraw[k, leaf]
                span = slice(leaf * width, (leaf + 1) * width)
                mboth[k, :cols, span] = raw * (1 - row)
                mboth[k, cols:, span] = raw * row
            return carry

        lax.fori_loop(0, XS, both, 0)

    leaf_rhs = rhs_ref[...]
    leaf_solve = leaf_products(leaf_rhs, inv_ref, 1)
    rhs_terms = by_parent(leaf_products(leaf_solve, masked, 0))
    diag_rows = jnp.concatenate(
        [
            jnp.sum(masked[leaf].astype(F32) * solved[leaf].astype(F32), axis=0, keepdims=True)
            for leaf in range(leaves)
        ],
        axis=0,
    )
    opening = jnp.concatenate([rhs_terms, by_parent(diag_rows)], axis=0)
    pl.semaphore_wait(barrier, 2 * (ZS - 1) + (SCENS - 1) + XS)

    scen_send(first, opening, f_send, f_recv)

    to_x = 2 * lax.rem(z, 2) + c
    lane = x // 2
    itself = jnp.logical_and(to_x == x, lane == c)
    for h in range(2):
        place = piece(mine, h, x)
        slot = a_recv.at[h, lax.rem(x, 2)]

        @pl.when(itself)
        def _():
            pltpu.make_async_copy(own.at[h], sbuf.at[place], slot).start()

        @pl.when(jnp.logical_not(itself))
        def _():
            put(own.at[h], sbuf.at[place], a_send, slot, (XS * y + to_x, 2 * z + lane))

    for d in (1, 3, 2):
        put(weight.at[x], weight.at[x], w_send, w_recv.at[x], (XS * y + lax.rem(x + d, XS), blk))

    start_own(0, 2)
    sums = collect(first, f_recv, SCENS)
    node_diag = ndiag_ref[...]
    reduced = nrhs_ref[...] - sums[0:2]
    scaling = node_diag + sums[2:4]
    state = reduced / scaling

    def sweep_a(it, value):
        blk_begin(it, leaf_products(of_parent(value), solved, 1))

    def sweep_b(it):
        inner = blk_collect(it)
        scen_send(u_at(it), by_parent(leaf_products(inner, masked, 0)), u_send, u_recv.at[it])

    def sweep_c(it, value):
        product_of = node_diag * value + collect(u_at(it), u_recv.at[it], SCENS)
        return value + DAMPING * (reduced - product_of) / scaling

    sweep_a(0, state)
    turn()
    blk_send(0)
    start_own(2, 5)
    sweep_b(0)
    spread(0, 2)
    start_own(5, 8)
    serve((0, 2), (0, 0))
    state = sweep_c(0, state)
    sweep_a(1, state)
    serve((2, 4), (0, 0))
    blk_send(1)
    serve((4, 5), (0, 0))
    sweep_b(1)
    spread(2, 4)
    serve((5, 7), (0, 2))
    state = sweep_c(1, state)
    sweep_a(2, state)
    serve((7, 8), (2, 5))
    blk_send(2)
    serve((8, 9), (5, 6))
    sweep_b(2)
    gathered()
    finish_own()
    serve((9, 11), (6, 8))
    shared((0, 8), (0, 8))
    product(near(0), (0, 1))
    ship_early(0)
    state = sweep_c(2, state)
    sweep_a(3, state)
    serve((11, 12), (8, 8))
    blk_send(3)
    product(near(1), (0, 1))
    ship_early(1)
    serve((12, 14), (8, 12))
    shared((8, 14), (8, 12))
    sweep_b(3)
    far_halves(0, both_acts)
    ship_own_late()
    ship_late(0)
    ship_late(1)
    serve((14, 16), (12, 14))
    shared((14, 16), (12, 14))
    far_halves(1, both_acts)
    state = sweep_c(3, state)
    node_ref[...] = state
    blk_begin(ITERS, leaf_products(of_parent(state), masked, 1))
    blk_send(ITERS)
    coupling = blk_collect(ITERS)
    leaf_ref[...] = leaf_products(leaf_rhs - coupling, inv_ref, 1)

    for d in (1, YS - 1):
        other = lax.rem(y + d, YS)
        wait(orecv.at[pl.ds(2 * other, 2)], o_recv.at[other])
    wait(narrow.at[pl.ds(2, 2)], n_recv)
    for h in range(2):
        total = obuf[y * 2 + h]
        for d in (1, YS - 1):
            total = total + orecv[lax.rem(y + d, YS) * 2 + h]
        total = total + narrow[2 + h].astype(F32)
        out_ref[0, :, h * half : (h + 1) * half] = total[:cols]
        out_ref[1, :, h * half : (h + 1) * half] = total[cols:]

    def drain(ref, count, sem):
        wait(ref.at[pl.ds(0, count)], sem)

    drain(first, SCENS - 1, f_send)
    drain(ubuf, ITERS * (SCENS - 1), u_send)
    drain(pair.at[:, 0], ITERS + 1, c_send)

    @pl.when(lax.rem(z + c, 2) == 1)
    def _():
        drain(tbuf, (ITERS + 1) * ZS, t_send)

    @pl.when(lax.rem(z + c, 2) == 0)
    def _():
        drain(tbuf, (ITERS + 1) * (ZS - 2), t_send)

    @pl.when(jnp.logical_not(itself))
    def _():
        drain(sbuf, 2, a_send)

    drain(weight, XS - 1, w_send)
    drain(mraw, XS - 1, m_send)

    @pl.when(source)
    def _():
        drain(sbuf, 16, z_send)
        drain(sbuf, 16, p_send)

    @pl.when(jnp.logical_not(source))
    def _():
        drain(sbuf, 12, z_send)
        drain(sbuf, 16, p_send)

    drain(obuf, 2 * (YS - 2), o_send)
    drain(narrow, 2, n_send)


def body(link, leaf_inverse, leaf_rhs, node_rhs, node_diag, parent, tile_mask):
    leaves, width, cols = link.shape
    nodes = node_rhs.shape[0]
    vmem = pl.BlockSpec(memory_space=pltpu.VMEM)
    smem = pl.BlockSpec(memory_space=pltpu.SMEM)
    dma = pltpu.SemaphoreType.DMA
    half = cols // 2
    return pl.pallas_call(
        step_kernel,
        out_shape=(
            jax.ShapeDtypeStruct((nodes, cols), F32),
            jax.ShapeDtypeStruct((leaves, width), F32),
            jax.ShapeDtypeStruct((nodes, cols, cols), F32),
        ),
        in_specs=[smem, smem] + [pl.BlockSpec(memory_space=pl.ANY)] * 2 + [vmem] * 3,
        out_specs=(vmem,) * 3,
        scratch_shapes=[
            pltpu.VMEM((leaves, width, cols), BF16),
            pltpu.VMEM((leaves, width, cols), BF16),
            pltpu.VMEM((SCENS, 2 * nodes, cols), F32),
            pltpu.VMEM((ITERS * SCENS, nodes, cols), F32),
            pltpu.VMEM(((ITERS + 1) * ZS, leaves, width), F32),
            pltpu.VMEM((ITERS + 1, 2, leaves, width), F32),
            pltpu.VMEM((2, leaves * width, half), BF16),
            pltpu.VMEM((2 * YS * XS, leaves * width, half), BF16),
            pltpu.VMEM((XS, leaves, cols, width), BF16),
            pltpu.VMEM((XS, 8, 128), F32),
            pltpu.VMEM((XS, nodes * cols, leaves * width), BF16),
            pltpu.VMEM((2 * YS, nodes * cols, half), F32),
            pltpu.VMEM((2 * YS, nodes * cols, half), F32),
            dma, dma, dma, dma((ITERS,)), dma, dma((ITERS + 1,)), dma, dma((ITERS + 1,)),
            dma, dma((2, 2)), dma, dma((XS,)), dma, dma((XS,)), dma, dma((16,)),
            dma, dma((16,)), dma((2, 2)), dma, dma((YS,)),
            pltpu.VMEM((4, nodes * cols, half), BF16), dma, dma,
            pltpu.VMEM((leaves, width, cols), BF16),
            pltpu.VMEM((leaves, width, width), BF16),
            dma((2,)),
        ],
        compiler_params=pltpu.CompilerParams(collective_id=0, has_side_effects=True, vmem_limit_bytes=60000 * 1024),
        name="step",
    )(parent, tile_mask.reshape(-1), link, leaf_inverse, leaf_rhs, node_rhs, node_diag)


def solution(mesh):
    in_specs = (
        P("scen", None, "blk"),
        P("scen", None, None),
        P("scen", None),
        P(None, "blk"),
        P(None, "blk"),
        P("scen"),
        P("scen", "blk"),
    )
    out_specs = (P(None, "blk"), P("scen", None), P(None, "blk", "scen"))
    return jax.shard_map(body, mesh=mesh, in_specs=in_specs, out_specs=out_specs, check_vma=False)
```

```python
import jax
import jax.numpy as jnp
from jax import lax
from jax.experimental import pallas as pl
from jax.experimental.pallas import tpu as pltpu
from jax.sharding import PartitionSpec as P

ITERS = 4
DAMPING = 0.4
MESH = pl.DeviceIdType.MESH
F32 = jnp.float32
BF16 = jnp.bfloat16
XS = 4
YS = 4
ZS = 8
SCENS = XS * YS


def split_rows(v):
    hi = v.astype(BF16).astype(F32)
    rest = v - hi
    mid = rest.astype(BF16).astype(F32)
    low = rest - mid
    return jnp.concatenate([hi, mid, low, jnp.zeros_like(v)], axis=0).astype(BF16)


def leaf_products(v, mats_ref, contract):
    parts = split_rows(v)
    leaves = mats_ref.shape[0]
    row = lax.broadcasted_iota(jnp.int32, v.shape, 0)
    total = jnp.zeros(v.shape, F32)
    for leaf in range(leaves):
        out = lax.dot_general(
            parts, mats_ref[leaf], (((1,), (contract,)), ((), ())), preferred_element_type=F32
        )
        out = out[0:4] + out[4:8] + out[8:12]
        total = total + jnp.where(row == leaf, out, 0.0)
    return total


def step_kernel(
    parent_ref, mask_ref, link_in, inv_in, rhs_ref, nrhs_ref, ndiag_ref,
    small_ref, out_ref,
    masked, solved, first, ubuf, tbuf, pair,
    own, sbuf, mraw, weight, mboth, obuf, orecv,
    f_send, f_recv, u_send, u_recv, t_send, t_recv, c_send, c_recv,
    a_send, a_recv, m_send, m_recv, w_send, w_recv, z_send, z_recv,
    p_send, p_recv, q_recv, o_send, o_recv, narrow, n_send, n_recv, lean, lean_in, l_send, l_recv, link_ref, inv_ref, in_sem,
):
    fetch_inv = pltpu.make_async_copy(inv_in, inv_ref, in_sem.at[0])
    fetch_inv.start()
    fetch_link = pltpu.make_async_copy(link_in, link_ref, in_sem.at[1])
    fetch_link.start()
    scen = lax.axis_index("scen")
    blk = lax.axis_index("blk")
    y, x = scen // XS, lax.rem(scen, XS)
    z, c = blk // 2, lax.rem(blk, 2)
    leaves, width, cols = link_ref.shape
    half = cols // 2
    source = lax.rem(z, 2) == x // 2
    partner = (scen, 2 * z + 1 - c)
    barrier = pltpu.get_barrier_semaphore()

    def greet(s, b):
        pl.semaphore_signal(barrier, inc=1, device_id=(s, b), device_id_type=MESH)

    for d in range(1, ZS):
        for e in range(2):
            greet(scen, 2 * lax.rem(z + d, ZS) + e)
    for d in range(1, SCENS):
        greet(lax.rem(scen + d, SCENS), blk)
    for d in range(XS):
        greet(XS * y + lax.rem(x + d, XS), 2 * z + 1 - c)

    def put(src, dst, send, recv, target):
        pltpu.make_async_remote_copy(
            src_ref=src, dst_ref=dst, send_sem=send, recv_sem=recv, device_id=target, device_id_type=MESH
        ).start()

    def wait(ref, sem):
        pltpu.make_async_copy(ref, ref, sem).wait()

    fetch_inv.wait()
    fetch_link.wait()
    for leaf in range(leaves):
        m = link_ref[leaf] * mask_ref[leaf].astype(BF16)
        s = jnp.dot(inv_ref[leaf], m, preferred_element_type=F32).astype(BF16)
        masked[leaf] = m
        solved[leaf] = s
        for h in range(2):
            own[h, leaf * width : (leaf + 1) * width, :] = s[:, h * half : (h + 1) * half]
    owner = [parent_ref[leaf].astype(F32) for leaf in range(leaves)]
    weight[x] = jnp.concatenate(
        [jnp.full((1, 128), owner[leaf], F32) for leaf in range(leaves)] + [jnp.zeros((8 - leaves, 128), F32)],
        axis=0,
    )

    row2 = lax.broadcasted_iota(jnp.int32, nrhs_ref.shape, 0)
    row4 = lax.broadcasted_iota(jnp.int32, rhs_ref.shape, 0)

    def by_parent(rows):
        total = jnp.zeros(nrhs_ref.shape, F32)
        for leaf in range(leaves):
            share_of = jnp.where(row2 == 0, 1.0 - owner[leaf], owner[leaf])
            total = total + share_of * rows[leaf : leaf + 1]
        return total

    def of_parent(values):
        total = jnp.zeros(rhs_ref.shape, F32)
        for leaf in range(leaves):
            mine = values[0:1] * (1.0 - owner[leaf]) + values[1:2] * owner[leaf]
            total = total + jnp.where(row4 == leaf, mine, 0.0)
        return total

    def scen_send(buf, value, send, recv):
        buf[scen] = value
        for d in range(1, SCENS):
            put(buf.at[scen], buf.at[scen], send, recv, (lax.rem(scen + d, SCENS), blk))

    def collect(buf, recv, count):
        wait(buf.at[pl.ds(0, count - 1)], recv)
        total = buf[0]
        for j in range(1, count):
            total = total + buf[j]
        return total

    def blk_begin(it, value):
        pair[it, c] = value
        put(pair.at[it, c], pair.at[it, c], c_send, c_recv.at[it], partner)

    def blk_send(it):
        wait(pair.at[it, 0], c_recv.at[it])
        at = ZS * it + z
        tbuf[at] = pair[it, 0] + pair[it, 1]
        for d in range(1, ZS // 2 + 1):
            to = lax.rem(z + jnp.where(c == 0, ZS - d, d), ZS)

            def both_cores():
                for e in range(2):
                    put(tbuf.at[at], tbuf.at[at], t_send, t_recv.at[it], (scen, 2 * to + e))

            if d < ZS // 2:
                both_cores()
            else:
                pl.when(lax.rem(z + c, 2) == 1)(both_cores)

    def blk_collect(it):
        return collect(tbuf.at[pl.ds(ZS * it, ZS)], t_recv.at[it], ZS)

    def u_at(it):
        return ubuf.at[pl.ds(SCENS * it, SCENS)]

    def piece(m, h, k):
        return (m * 2 + h) * XS + k

    def ring(place, step):
        to = lax.rem(z + jnp.where(c == 0, 1, ZS - 1), ZS)
        put(sbuf.at[place], sbuf.at[place], z_send, z_recv.at[step], (scen, 2 * to + c))

    def share(place, slot):
        put(sbuf.at[place], sbuf.at[place], p_send, slot, partner)

    mine = z // 2

    beside = x + 1 - 2 * lax.rem(x, 2)

    def order(q):
        h = jnp.where(jnp.logical_or(q == 1, q >= 5), 1, 0)
        j = jnp.where(q < 2, 0, jnp.where(q < 5, q - 1, q - 4))
        k = jnp.where(j == 0, x, jnp.where(j == 1, beside, lax.rem(jnp.where(j == 2, beside, x) + 2, XS)))
        return h, k

    def far_order(way, p):
        return jnp.where(way == 0, p, jnp.where(p < 2, p, jnp.where(p < 6, p + 2, p - 4)))

    def crosses(way, p):
        return jnp.logical_and(p >= 2 * way, p < 4 + 2 * way)

    def start_own(begin, end):
        @pl.when(source)
        def _():
            for q in range(begin, end):
                h, k = order(q)
                place = piece(mine, h, k)
                direct = k // 2 == c

                @pl.when(direct)
                def _():
                    wait(sbuf.at[place], a_recv.at[h, lax.rem(k, 2)])
                    ring(place, q)
                    share(place, q_recv.at[h, lax.rem(k, 2)])

                @pl.when(jnp.logical_not(direct))
                def _():
                    wait(sbuf.at[place], q_recv.at[h, lax.rem(k, 2)])
                    ring(place, q)

    def arrival(way, n):
        far = n // 8
        p = lax.rem(n, 8)
        away = jnp.where(source, 2, 1) + 2 * far
        at = lax.rem(z + jnp.where(way == 0, ZS - away, away), ZS)
        h, k = order(jnp.where(far == 0, p, far_order(way, p)))
        comes = jnp.logical_or(jnp.logical_not(source), jnp.logical_or(far == 0, crosses(way, p)))
        return piece(at // 2, h, k), at // 2, comes

    def serve(plain_range, source_range):
        begin = jnp.where(source, source_range[0], plain_range[0])
        end = jnp.where(source, source_range[1], plain_range[1])

        def one(n, carry):
            place, at, comes = arrival(c, n)
            far = n // 8
            p = lax.rem(n, 8)

            @pl.when(comes)
            def _():
                wait(sbuf.at[place], z_recv.at[n])

                @pl.when(jnp.logical_and(jnp.logical_not(source), jnp.logical_or(far == 0, crosses(c, p))))
                def _():
                    ring(place, n)

                @pl.when(jnp.logical_and(source, far == 0))
                def _():
                    @pl.when(jnp.logical_or(c == 0, p < 2))
                    def _():
                        ring(place, n + 8)

                    @pl.when(jnp.logical_and(c == 1, p >= 4))
                    def _():
                        ring(place, n + 6)

                    @pl.when(jnp.logical_and(c == 1, p == 7))
                    def _():
                        for q in (2, 3):
                            ring(piece(at, *order(q)), 12 + q)

                share(place, p_recv.at[n])

            return carry

        lax.fori_loop(begin, end, one, 0)

    def shared(plain_range, source_range):
        begin = jnp.where(source, source_range[0], plain_range[0])
        end = jnp.where(source, source_range[1], plain_range[1])

        def one(n, carry):
            place, at, comes = arrival(1 - c, n)

            @pl.when(comes)
            def _():
                wait(sbuf.at[place], p_recv.at[n])

            return carry

        lax.fori_loop(begin, end, one, 0)

    def product(m, halves):
        def over(k, carry):
            right = [sbuf[piece(m, h, k)] for h in halves]
            right = right[0] if len(right) == 1 else jnp.concatenate(right, axis=1)
            out = jnp.dot(mboth[k], right, preferred_element_type=F32)
            for i, h in enumerate(halves):
                part = out[:, i * half : (i + 1) * half]
                obuf[m * 2 + h] = jnp.where(k == 0, part, obuf[m * 2 + h] + part)
            return carry

        lax.fori_loop(0, XS, over, 0)

    across = lax.rem(y + 2, YS)

    def ship(m, halves):
        @pl.when(jnp.logical_and(m != y, m != across))
        def _():
            for h in halves:
                put(obuf.at[m * 2 + h], orecv.at[y * 2 + h], o_send, o_recv.at[y], (XS * m + x, blk))

        @pl.when(m == across)
        def _():
            for h in halves:
                narrow[h] = obuf[m * 2 + h].astype(BF16)
                put(narrow.at[h], narrow.at[2 + h], n_send, n_recv, (XS * m + x, blk))

    def leaves_by(m):
        away = lax.rem(m - y + YS, YS)
        up = jnp.logical_or(away == 1, jnp.logical_and(away == 2, lax.rem(y, 2) == 0))
        return jnp.where(away == 0, 0, jnp.where(up, 1, 2))

    def near(way):
        away = jnp.where(source, 2, 1)
        return lax.rem(z + (ZS - away if way == 0 else away), ZS) // 2

    def free_for(way):
        link = leaves_by(near(way))
        taken = jnp.logical_and(source, link == leaves_by(mine))
        if way == 1:
            taken = jnp.logical_or(taken, link == leaves_by(near(0)))
        return jnp.logical_not(taken)

    def ship_early(way, at_source=True):
        @pl.when(jnp.logical_and(free_for(way), jnp.logical_or(at_source, jnp.logical_not(source))))
        def _():
            ship(near(way), (0,))

    def ship_own_late():
        @pl.when(source)
        def _():
            ship(mine, (1,))

    def ship_late(way, at_source=True):
        @pl.when(jnp.logical_not(jnp.logical_and(free_for(way), jnp.logical_or(at_source, jnp.logical_not(source)))))
        def _():
            ship(near(way), (0,))

        ship(near(way), (1,))

    def finish_own():
        @pl.when(source)
        def _():
            product(mine, (0, 1))
            ship(mine, (0,))

    def far_halves(i, act):
        def one(way, carry):
            m = lax.rem(z + jnp.where(way == 0, ZS - 3, 3), ZS) // 2

            @pl.when(jnp.logical_not(source))
            def _():
                for h in range(2):
                    @pl.when(way == (i + h) % 2)
                    def _():
                        act(m, (h,))

            return carry

        lax.fori_loop(0, 2, one, 0)

        @pl.when(source)
        def _():
            act(lax.rem(z + 4, ZS) // 2, (i,))

    def both_acts(m, halves):
        product(m, halves)
        ship(m, halves)

    def last_acts(m, halves):
        product(m, halves)
        h = halves[0]

        @pl.when(m != y)
        def _():
            lean[lax.rem(m - y + YS, YS)] = obuf[m * 2 + h].astype(BF16)

        @pl.when(m == across)
        def _():
            put(lean.at[2], narrow.at[2 + h], n_send, n_recv, (XS * m + x, blk))

        @pl.when(jnp.logical_and(m != y, m != across))
        def _():
            put(lean.at[lax.rem(m - y + YS, YS)], lean_in.at[y], l_send, l_recv.at[y], (XS * m + x, blk))

    def spread(begin, end):
        for leaf in range(begin, end):
            for d in (1, 3, 2):
                put(mraw.at[x, leaf], mraw.at[x, leaf], m_send, m_recv.at[x], (XS * y + lax.rem(x + d, XS), blk))

    def turn():
        for leaf in range(leaves):
            mraw[x, leaf] = masked[leaf].astype(F32).T.astype(BF16)

    def gathered():
        for d in range(1, XS):
            other = lax.rem(x + d, XS)
            wait(weight.at[other], w_recv.at[other])
            wait(mraw.at[other], m_recv.at[other])

        def both(k, carry):
            w = weight[k]
            for leaf in range(leaves):
                row = jnp.concatenate([w[leaf : leaf + 1]] * (width // 128), axis=1).astype(BF16)
                raw = mraw[k, leaf]
                span = slice(leaf * width, (leaf + 1) * width)
                mboth[k, :cols, span] = raw * (1 - row)
                mboth[k, cols:, span] = raw * row
            return carry

        lax.fori_loop(0, XS, both, 0)

    leaf_rhs = rhs_ref[...]
    leaf_solve = leaf_products(leaf_rhs, inv_ref, 1)
    rhs_terms = by_parent(leaf_products(leaf_solve, masked, 0))
    diag_rows = jnp.concatenate(
        [
            jnp.sum(masked[leaf].astype(F32) * solved[leaf].astype(F32), axis=0, keepdims=True)
            for leaf in range(leaves)
        ],
        axis=0,
    )
    opening = jnp.concatenate([rhs_terms, by_parent(diag_rows)], axis=0)
    pl.semaphore_wait(barrier, 2 * (ZS - 1) + (SCENS - 1) + XS)

    scen_send(first, opening, f_send, f_recv)

    to_x = 2 * lax.rem(z, 2) + c
    lane = x // 2
    itself = jnp.logical_and(to_x == x, lane == c)
    for h in range(2):
        place = piece(mine, h, x)
        slot = a_recv.at[h, lax.rem(x, 2)]

        @pl.when(itself)
        def _():
            pltpu.make_async_copy(own.at[h], sbuf.at[place], slot).start()

        @pl.when(jnp.logical_not(itself))
        def _():
            put(own.at[h], sbuf.at[place], a_send, slot, (XS * y + to_x, 2 * z + lane))

    for d in (1, 3, 2):
        put(weight.at[x], weight.at[x], w_send, w_recv.at[x], (XS * y + lax.rem(x + d, XS), blk))

    start_own(0, 2)
    sums = collect(first, f_recv, SCENS)
    node_diag = ndiag_ref[...]
    reduced = nrhs_ref[...] - sums[0:2]
    scaling = node_diag + sums[2:4]
    state = reduced / scaling

    def sweep_a(it, value):
        blk_begin(it, leaf_products(of_parent(value), solved, 1))

    def sweep_b(it):
        inner = blk_collect(it)
        scen_send(u_at(it), by_parent(leaf_products(inner, masked, 0)), u_send, u_recv.at[it])

    def sweep_c(it, value):
        product_of = node_diag * value + collect(u_at(it), u_recv.at[it], SCENS)
        return value + DAMPING * (reduced - product_of) / scaling

    sweep_a(0, state)
    turn()
    blk_send(0)
    start_own(2, 5)
    sweep_b(0)
    spread(0, 2)
    start_own(5, 8)
    serve((0, 2), (0, 0))
    state = sweep_c(0, state)
    sweep_a(1, state)
    serve((2, 4), (0, 0))
    blk_send(1)
    serve((4, 5), (0, 0))
    sweep_b(1)
    spread(2, 4)
    serve((5, 7), (0, 2))
    state = sweep_c(1, state)
    sweep_a(2, state)
    serve((7, 8), (2, 5))
    blk_send(2)
    serve((8, 9), (5, 6))
    sweep_b(2)
    gathered()
    finish_own()
    serve((9, 11), (6, 8))
    shared((0, 8), (0, 8))
    product(near(0), (0, 1))
    ship_early(0)
    state = sweep_c(2, state)
    sweep_a(3, state)
    serve((11, 12), (8, 8))
    blk_send(3)
    product(near(1), (0, 1))
    ship_early(1)
    serve((12, 14), (8, 12))
    shared((8, 14), (8, 12))
    sweep_b(3)
    far_halves(0, both_acts)
    ship_own_late()
    ship_late(0)
    ship_late(1)
    serve((14, 16), (12, 14))
    shared((14, 16), (12, 14))
    far_halves(1, last_acts)
    state = sweep_c(3, state)
    small_ref[0:2, :] = state
    blk_begin(ITERS, leaf_products(of_parent(state), masked, 1))
    blk_send(ITERS)
    coupling = blk_collect(ITERS)
    small_ref[2:6, :] = leaf_products(leaf_rhs - coupling, inv_ref, 1)

    away_0 = lax.rem(z + ZS - 3, ZS) // 2
    away_1 = lax.rem(z + 3, ZS) // 2
    farthest = lax.rem(z + 4, ZS) // 2
    last_half = jnp.where(
        source, jnp.where(farthest == y, 1, 2), jnp.where(away_0 == y, 1, jnp.where(away_1 == y, 0, 2))
    )
    for d in (1, YS - 1):
        other = lax.rem(y + d, YS)

        @pl.when(last_half == 2)
        def _():
            wait(orecv.at[pl.ds(2 * other, 2)], o_recv.at[other])

        @pl.when(last_half < 2)
        def _():
            wait(orecv.at[2 * other + 1 - last_half], o_recv.at[other])
            wait(lean_in.at[other], l_recv.at[other])
            orecv[2 * other + last_half] = lean_in[other].astype(F32)

    wait(narrow.at[pl.ds(2, 2)], n_recv)
    for h in range(2):
        total = obuf[y * 2 + h]
        for d in (1, YS - 1):
            total = total + orecv[lax.rem(y + d, YS) * 2 + h]
        total = total + narrow[2 + h].astype(F32)
        out_ref[0, :, h * half : (h + 1) * half] = total[:cols]
        out_ref[1, :, h * half : (h + 1) * half] = total[cols:]

    def drain(ref, count, sem):
        wait(ref.at[pl.ds(0, count)], sem)

    drain(first, SCENS - 1, f_send)
    drain(ubuf, ITERS * (SCENS - 1), u_send)
    drain(pair.at[:, 0], ITERS + 1, c_send)

    @pl.when(lax.rem(z + c, 2) == 1)
    def _():
        drain(tbuf, (ITERS + 1) * ZS, t_send)

    @pl.when(lax.rem(z + c, 2) == 0)
    def _():
        drain(tbuf, (ITERS + 1) * (ZS - 2), t_send)

    @pl.when(jnp.logical_not(itself))
    def _():
        drain(sbuf, 2, a_send)

    drain(weight, XS - 1, w_send)
    drain(mraw, XS - 1, m_send)

    @pl.when(source)
    def _():
        drain(sbuf, 16, z_send)
        drain(sbuf, 16, p_send)

    @pl.when(jnp.logical_not(source))
    def _():
        drain(sbuf, 12, z_send)
        drain(sbuf, 16, p_send)

    drain(narrow, 2, n_send)
    def neighbour(m):
        return jnp.where(jnp.logical_or(lax.rem(m - y + YS, YS) == 1, lax.rem(m - y + YS, YS) == 3), 1, 0)

    lean_count = jnp.where(source, neighbour(farthest), neighbour(away_0) + neighbour(away_1))
    for count in range(3):

        @pl.when(lean_count == count)
        def _():
            drain(obuf, 2 * (YS - 2) - count, o_send)
            if count:
                drain(lean_in, count, l_send)


def body(link, leaf_inverse, leaf_rhs, node_rhs, node_diag, parent, tile_mask):
    leaves, width, cols = link.shape
    nodes = node_rhs.shape[0]
    vmem = pl.BlockSpec(memory_space=pltpu.VMEM)
    smem = pl.BlockSpec(memory_space=pltpu.SMEM)
    dma = pltpu.SemaphoreType.DMA
    half = cols // 2
    small, schur_out = pl.pallas_call(
        step_kernel,
        out_shape=(
            jax.ShapeDtypeStruct((8, cols), F32),
            jax.ShapeDtypeStruct((nodes, cols, cols), F32),
        ),
        in_specs=[smem, smem] + [pl.BlockSpec(memory_space=pl.ANY)] * 2 + [vmem] * 3,
        out_specs=(vmem,) * 2,
        scratch_shapes=[
            pltpu.VMEM((leaves, width, cols), BF16),
            pltpu.VMEM((leaves, width, cols), BF16),
            pltpu.VMEM((SCENS, 2 * nodes, cols), F32),
            pltpu.VMEM((ITERS * SCENS, nodes, cols), F32),
            pltpu.VMEM(((ITERS + 1) * ZS, leaves, width), F32),
            pltpu.VMEM((ITERS + 1, 2, leaves, width), F32),
            pltpu.VMEM((2, leaves * width, half), BF16),
            pltpu.VMEM((2 * YS * XS, leaves * width, half), BF16),
            pltpu.VMEM((XS, leaves, cols, width), BF16),
            pltpu.VMEM((XS, 8, 128), F32),
            pltpu.VMEM((XS, nodes * cols, leaves * width), BF16),
            pltpu.VMEM((2 * YS, nodes * cols, half), F32),
            pltpu.VMEM((2 * YS, nodes * cols, half), F32),
            dma, dma, dma, dma((ITERS,)), dma, dma((ITERS + 1,)), dma, dma((ITERS + 1,)),
            dma, dma((2, 2)), dma, dma((XS,)), dma, dma((XS,)), dma, dma((16,)),
            dma, dma((16,)), dma((2, 2)), dma, dma((YS,)),
            pltpu.VMEM((4, nodes * cols, half), BF16), dma, dma,
            pltpu.VMEM((YS, nodes * cols, half), BF16),
            pltpu.VMEM((YS, nodes * cols, half), BF16), dma, dma((YS,)),
            pltpu.VMEM((leaves, width, cols), BF16),
            pltpu.VMEM((leaves, width, width), BF16),
            dma((2,)),
        ],
        compiler_params=pltpu.CompilerParams(collective_id=0, has_side_effects=True, vmem_limit_bytes=60000 * 1024),
        name="step",
    )(parent, tile_mask.reshape(-1), link, leaf_inverse, leaf_rhs, node_rhs, node_diag)
    return small[:nodes], small[nodes : nodes + leaves], schur_out


def solution(mesh):
    in_specs = (
        P("scen", None, "blk"),
        P("scen", None, None),
        P("scen", None),
        P(None, "blk"),
        P(None, "blk"),
        P("scen"),
        P("scen", "blk"),
    )
    out_specs = (P(None, "blk"), P("scen", None), P(None, "blk", "scen"))
    return jax.shard_map(body, mesh=mesh, in_specs=in_specs, out_specs=out_specs, check_vma=False)
```

```python
import jax
import jax.numpy as jnp
from jax import lax
from jax.experimental import pallas as pl
from jax.experimental.pallas import tpu as pltpu
from jax.sharding import PartitionSpec as P

ITERS = 4
DAMPING = 0.4
MESH = pl.DeviceIdType.MESH
F32 = jnp.float32
BF16 = jnp.bfloat16
XS = 4
YS = 4
ZS = 8
SCENS = XS * YS


def split_rows(v):
    hi = v.astype(BF16).astype(F32)
    rest = v - hi
    mid = rest.astype(BF16).astype(F32)
    low = rest - mid
    return jnp.concatenate([hi, mid, low, jnp.zeros_like(v)], axis=0).astype(BF16)


def leaf_products(v, mats_ref, contract):
    parts = split_rows(v)
    leaves = mats_ref.shape[0]
    row = lax.broadcasted_iota(jnp.int32, v.shape, 0)
    total = jnp.zeros(v.shape, F32)
    for leaf in range(leaves):
        out = lax.dot_general(
            parts, mats_ref[leaf], (((1,), (contract,)), ((), ())), preferred_element_type=F32
        )
        out = out[0:4] + out[4:8] + out[8:12]
        total = total + jnp.where(row == leaf, out, 0.0)
    return total


def step_kernel(
    parent_ref, mask_ref, link_in, inv_in, rhs_ref, nrhs_ref, ndiag_ref,
    node_ref, leaf_ref, out_ref,
    masked, solved, first, ubuf, tbuf, pair,
    own, sbuf, mraw, weight, mboth, obuf, orecv,
    f_send, f_recv, u_send, u_recv, t_send, t_recv, c_send, c_recv,
    a_send, a_recv, m_send, m_recv, w_send, w_recv, z_send, z_recv,
    p_send, p_recv, q_recv, o_send, o_recv, narrow, n_send, n_recv, lean, lean_in, l_send, l_recv, link_ref, inv_ref, in_sem,
):
    fetch_inv = pltpu.make_async_copy(inv_in, inv_ref, in_sem.at[0])
    fetch_inv.start()
    fetch_link = pltpu.make_async_copy(link_in, link_ref, in_sem.at[1])
    fetch_link.start()
    scen = lax.axis_index("scen")
    blk = lax.axis_index("blk")
    y, x = scen // XS, lax.rem(scen, XS)
    z, c = blk // 2, lax.rem(blk, 2)
    leaves, width, cols = link_ref.shape
    half = cols // 2
    source = lax.rem(z, 2) == x // 2
    partner = (scen, 2 * z + 1 - c)
    barrier = pltpu.get_barrier_semaphore()

    def greet(s, b):
        pl.semaphore_signal(barrier, inc=1, device_id=(s, b), device_id_type=MESH)

    for d in range(1, ZS):
        for e in range(2):
            greet(scen, 2 * lax.rem(z + d, ZS) + e)
    for d in range(1, SCENS):
        greet(lax.rem(scen + d, SCENS), blk)
    for d in range(XS):
        greet(XS * y + lax.rem(x + d, XS), 2 * z + 1 - c)

    def put(src, dst, send, recv, target):
        pltpu.make_async_remote_copy(
            src_ref=src, dst_ref=dst, send_sem=send, recv_sem=recv, device_id=target, device_id_type=MESH
        ).start()

    def wait(ref, sem):
        pltpu.make_async_copy(ref, ref, sem).wait()

    fetch_inv.wait()
    fetch_link.wait()
    for leaf in range(leaves):
        m = link_ref[leaf] * mask_ref[leaf].astype(BF16)
        s = jnp.dot(inv_ref[leaf], m, preferred_element_type=F32).astype(BF16)
        masked[leaf] = m
        solved[leaf] = s
        for h in range(2):
            own[h, leaf * width : (leaf + 1) * width, :] = s[:, h * half : (h + 1) * half]
    owner = [parent_ref[leaf].astype(F32) for leaf in range(leaves)]
    weight[x] = jnp.concatenate(
        [jnp.full((1, 128), owner[leaf], F32) for leaf in range(leaves)] + [jnp.zeros((8 - leaves, 128), F32)],
        axis=0,
    )

    row2 = lax.broadcasted_iota(jnp.int32, nrhs_ref.shape, 0)
    row4 = lax.broadcasted_iota(jnp.int32, rhs_ref.shape, 0)

    def by_parent(rows):
        total = jnp.zeros(nrhs_ref.shape, F32)
        for leaf in range(leaves):
            share_of = jnp.where(row2 == 0, 1.0 - owner[leaf], owner[leaf])
            total = total + share_of * rows[leaf : leaf + 1]
        return total

    def of_parent(values):
        total = jnp.zeros(rhs_ref.shape, F32)
        for leaf in range(leaves):
            mine = values[0:1] * (1.0 - owner[leaf]) + values[1:2] * owner[leaf]
            total = total + jnp.where(row4 == leaf, mine, 0.0)
        return total

    def scen_send(buf, value, send, recv):
        buf[scen] = value
        for d in range(1, SCENS):
            put(buf.at[scen], buf.at[scen], send, recv, (lax.rem(scen + d, SCENS), blk))

    def collect(buf, recv, count):
        wait(buf.at[pl.ds(0, count - 1)], recv)
        total = buf[0]
        for j in range(1, count):
            total = total + buf[j]
        return total

    def blk_begin(it, value):
        pair[it, c] = value
        put(pair.at[it, c], pair.at[it, c], c_send, c_recv.at[it], partner)

    def blk_send(it):
        wait(pair.at[it, 0], c_recv.at[it])
        at = ZS * it + z
        tbuf[at] = pair[it, 0] + pair[it, 1]
        for d in range(1, ZS // 2 + 1):
            to = lax.rem(z + jnp.where(c == 0, ZS - d, d), ZS)

            def both_cores():
                for e in range(2):
                    put(tbuf.at[at], tbuf.at[at], t_send, t_recv.at[it], (scen, 2 * to + e))

            if d < ZS // 2:
                both_cores()
            else:
                pl.when(lax.rem(z + c, 2) == 1)(both_cores)

    def blk_collect(it):
        return collect(tbuf.at[pl.ds(ZS * it, ZS)], t_recv.at[it], ZS)

    def u_at(it):
        return ubuf.at[pl.ds(SCENS * it, SCENS)]

    def piece(m, h, k):
        return (m * 2 + h) * XS + k

    def ring(place, step):
        to = lax.rem(z + jnp.where(c == 0, 1, ZS - 1), ZS)
        put(sbuf.at[place], sbuf.at[place], z_send, z_recv.at[step], (scen, 2 * to + c))

    def share(place, slot):
        put(sbuf.at[place], sbuf.at[place], p_send, slot, partner)

    mine = z // 2

    beside = x + 1 - 2 * lax.rem(x, 2)

    def order(q):
        h = jnp.where(jnp.logical_or(q == 1, q >= 5), 1, 0)
        j = jnp.where(q < 2, 0, jnp.where(q < 5, q - 1, q - 4))
        k = jnp.where(j == 0, x, jnp.where(j == 1, beside, lax.rem(jnp.where(j == 2, beside, x) + 2, XS)))
        return h, k

    def far_order(way, p):
        return jnp.where(way == 0, p, jnp.where(p < 2, p, jnp.where(p < 6, p + 2, p - 4)))

    def crosses(way, p):
        return jnp.logical_and(p >= 2 * way, p < 4 + 2 * way)

    def start_own(begin, end):
        @pl.when(source)
        def _():
            for q in range(begin, end):
                h, k = order(q)
                place = piece(mine, h, k)
                direct = k // 2 == c

                @pl.when(direct)
                def _():
                    wait(sbuf.at[place], a_recv.at[h, lax.rem(k, 2)])
                    ring(place, q)
                    share(place, q_recv.at[h, lax.rem(k, 2)])

                @pl.when(jnp.logical_not(direct))
                def _():
                    wait(sbuf.at[place], q_recv.at[h, lax.rem(k, 2)])
                    ring(place, q)

    def arrival(way, n):
        far = n // 8
        p = lax.rem(n, 8)
        away = jnp.where(source, 2, 1) + 2 * far
        at = lax.rem(z + jnp.where(way == 0, ZS - away, away), ZS)
        h, k = order(jnp.where(far == 0, p, far_order(way, p)))
        comes = jnp.logical_or(jnp.logical_not(source), jnp.logical_or(far == 0, crosses(way, p)))
        return piece(at // 2, h, k), at // 2, comes

    def serve(plain_range, source_range):
        begin = jnp.where(source, source_range[0], plain_range[0])
        end = jnp.where(source, source_range[1], plain_range[1])

        def one(n, carry):
            place, at, comes = arrival(c, n)
            far = n // 8
            p = lax.rem(n, 8)

            @pl.when(comes)
            def _():
                wait(sbuf.at[place], z_recv.at[n])

                @pl.when(jnp.logical_and(jnp.logical_not(source), jnp.logical_or(far == 0, crosses(c, p))))
                def _():
                    ring(place, n)

                @pl.when(jnp.logical_and(source, far == 0))
                def _():
                    @pl.when(jnp.logical_or(c == 0, p < 2))
                    def _():
                        ring(place, n + 8)

                    @pl.when(jnp.logical_and(c == 1, p >= 4))
                    def _():
                        ring(place, n + 6)

                    @pl.when(jnp.logical_and(c == 1, p == 7))
                    def _():
                        for q in (2, 3):
                            ring(piece(at, *order(q)), 12 + q)

                share(place, p_recv.at[n])

            return carry

        lax.fori_loop(begin, end, one, 0)

    def shared(plain_range, source_range):
        begin = jnp.where(source, source_range[0], plain_range[0])
        end = jnp.where(source, source_range[1], plain_range[1])

        def one(n, carry):
            place, at, comes = arrival(1 - c, n)

            @pl.when(comes)
            def _():
                wait(sbuf.at[place], p_recv.at[n])

            return carry

        lax.fori_loop(begin, end, one, 0)

    def product(m, halves):
        def over(k, carry):
            right = [sbuf[piece(m, h, k)] for h in halves]
            right = right[0] if len(right) == 1 else jnp.concatenate(right, axis=1)
            out = jnp.dot(mboth[k], right, preferred_element_type=F32)
            for i, h in enumerate(halves):
                part = out[:, i * half : (i + 1) * half]
                obuf[m * 2 + h] = jnp.where(k == 0, part, obuf[m * 2 + h] + part)
            return carry

        lax.fori_loop(0, XS, over, 0)

    across = lax.rem(y + 2, YS)

    def ship(m, halves):
        @pl.when(jnp.logical_and(m != y, m != across))
        def _():
            for h in halves:
                put(obuf.at[m * 2 + h], orecv.at[y * 2 + h], o_send, o_recv.at[y], (XS * m + x, blk))

        @pl.when(m == across)
        def _():
            for h in halves:
                narrow[h] = obuf[m * 2 + h].astype(BF16)
                put(narrow.at[h], narrow.at[2 + h], n_send, n_recv, (XS * m + x, blk))

    def leaves_by(m):
        away = lax.rem(m - y + YS, YS)
        up = jnp.logical_or(away == 1, jnp.logical_and(away == 2, lax.rem(y, 2) == 0))
        return jnp.where(away == 0, 0, jnp.where(up, 1, 2))

    def near(way):
        away = jnp.where(source, 2, 1)
        return lax.rem(z + (ZS - away if way == 0 else away), ZS) // 2

    def free_for(way):
        link = leaves_by(near(way))
        taken = jnp.logical_and(source, link == leaves_by(mine))
        if way == 1:
            taken = jnp.logical_or(taken, link == leaves_by(near(0)))
        return jnp.logical_not(taken)

    def ship_early(way, at_source=True):
        @pl.when(jnp.logical_and(free_for(way), jnp.logical_or(at_source, jnp.logical_not(source))))
        def _():
            ship(near(way), (0,))

    def ship_own_late():
        @pl.when(source)
        def _():
            ship(mine, (1,))

    def ship_late(way, at_source=True):
        @pl.when(jnp.logical_not(jnp.logical_and(free_for(way), jnp.logical_or(at_source, jnp.logical_not(source)))))
        def _():
            ship(near(way), (0,))

        ship(near(way), (1,))

    def finish_own():
        @pl.when(source)
        def _():
            product(mine, (0, 1))
            ship(mine, (0,))

    def far_halves(i, act):
        def one(way, carry):
            m = lax.rem(z + jnp.where(way == 0, ZS - 3, 3), ZS) // 2

            @pl.when(jnp.logical_not(source))
            def _():
                for h in range(2):
                    @pl.when(way == (i + h) % 2)
                    def _():
                        act(m, (h,))

            return carry

        lax.fori_loop(0, 2, one, 0)

        @pl.when(source)
        def _():
            act(lax.rem(z + 4, ZS) // 2, (i,))

    def both_acts(m, halves):
        product(m, halves)
        ship(m, halves)

    def last_acts(m, halves):
        product(m, halves)
        h = halves[0]

        @pl.when(m != y)
        def _():
            lean[lax.rem(m - y + YS, YS)] = obuf[m * 2 + h].astype(BF16)

        @pl.when(m == across)
        def _():
            put(lean.at[2], narrow.at[2 + h], n_send, n_recv, (XS * m + x, blk))

        @pl.when(jnp.logical_and(m != y, m != across))
        def _():
            put(lean.at[lax.rem(m - y + YS, YS)], lean_in.at[y], l_send, l_recv.at[y], (XS * m + x, blk))

    def spread(begin, end):
        for leaf in range(begin, end):
            for d in (1, 3, 2):
                put(mraw.at[x, leaf], mraw.at[x, leaf], m_send, m_recv.at[x], (XS * y + lax.rem(x + d, XS), blk))

    def turn():
        for leaf in range(leaves):
            mraw[x, leaf] = masked[leaf].astype(F32).T.astype(BF16)

    def gathered():
        for d in range(1, XS):
            other = lax.rem(x + d, XS)
            wait(weight.at[other], w_recv.at[other])
            wait(mraw.at[other], m_recv.at[other])

        def both(k, carry):
            w = weight[k]
            for leaf in range(leaves):
                row = jnp.concatenate([w[leaf : leaf + 1]] * (width // 128), axis=1).astype(BF16)
                raw = mraw[k, leaf]
                span = slice(leaf * width, (leaf + 1) * width)
                mboth[k, :cols, span] = raw * (1 - row)
                mboth[k, cols:, span] = raw * row
            return carry

        lax.fori_loop(0, XS, both, 0)

    leaf_rhs = rhs_ref[...]
    leaf_solve = leaf_products(leaf_rhs, inv_ref, 1)
    rhs_terms = by_parent(leaf_products(leaf_solve, masked, 0))
    diag_rows = jnp.concatenate(
        [
            jnp.sum(masked[leaf].astype(F32) * solved[leaf].astype(F32), axis=0, keepdims=True)
            for leaf in range(leaves)
        ],
        axis=0,
    )
    opening = jnp.concatenate([rhs_terms, by_parent(diag_rows)], axis=0)
    pl.semaphore_wait(barrier, 2 * (ZS - 1) + (SCENS - 1) + XS)

    scen_send(first, opening, f_send, f_recv)

    to_x = 2 * lax.rem(z, 2) + c
    lane = x // 2
    itself = jnp.logical_and(to_x == x, lane == c)
    for h in range(2):
        place = piece(mine, h, x)
        slot = a_recv.at[h, lax.rem(x, 2)]

        @pl.when(itself)
        def _():
            pltpu.make_async_copy(own.at[h], sbuf.at[place], slot).start()

        @pl.when(jnp.logical_not(itself))
        def _():
            put(own.at[h], sbuf.at[place], a_send, slot, (XS * y + to_x, 2 * z + lane))

    for d in (1, 3, 2):
        put(weight.at[x], weight.at[x], w_send, w_recv.at[x], (XS * y + lax.rem(x + d, XS), blk))

    start_own(0, 2)
    sums = collect(first, f_recv, SCENS)
    node_diag = ndiag_ref[...]
    reduced = nrhs_ref[...] - sums[0:2]
    scaling = node_diag + sums[2:4]
    state = reduced / scaling

    def sweep_a(it, value):
        blk_begin(it, leaf_products(of_parent(value), solved, 1))

    def sweep_b(it):
        inner = blk_collect(it)
        scen_send(u_at(it), by_parent(leaf_products(inner, masked, 0)), u_send, u_recv.at[it])

    def sweep_c(it, value):
        product_of = node_diag * value + collect(u_at(it), u_recv.at[it], SCENS)
        return value + DAMPING * (reduced - product_of) / scaling

    sweep_a(0, state)
    turn()
    blk_send(0)
    start_own(2, 5)
    sweep_b(0)
    spread(0, 2)
    start_own(5, 8)
    serve((0, 2), (0, 0))
    state = sweep_c(0, state)
    sweep_a(1, state)
    serve((2, 4), (0, 0))
    blk_send(1)
    serve((4, 5), (0, 0))
    sweep_b(1)
    spread(2, 4)
    serve((5, 7), (0, 2))
    state = sweep_c(1, state)
    sweep_a(2, state)
    serve((7, 8), (2, 5))
    blk_send(2)
    serve((8, 9), (5, 6))
    sweep_b(2)
    gathered()
    finish_own()
    serve((9, 11), (6, 8))
    shared((0, 8), (0, 8))
    product(near(0), (0, 1))
    ship_early(0)
    state = sweep_c(2, state)
    sweep_a(3, state)
    serve((11, 12), (8, 8))
    blk_send(3)
    product(near(1), (0, 1))
    ship_early(1)
    serve((12, 14), (8, 12))
    shared((8, 14), (8, 12))
    sweep_b(3)
    far_halves(0, both_acts)
    ship_own_late()
    ship_late(0)
    ship_late(1)
    serve((14, 16), (12, 14))
    shared((14, 16), (12, 14))
    state = sweep_c(3, state)
    node_ref[...] = state
    blk_begin(ITERS, leaf_products(of_parent(state), masked, 1))
    blk_send(ITERS)
    far_halves(1, last_acts)
    coupling = blk_collect(ITERS)
    leaf_ref[...] = leaf_products(leaf_rhs - coupling, inv_ref, 1)

    away_0 = lax.rem(z + ZS - 3, ZS) // 2
    away_1 = lax.rem(z + 3, ZS) // 2
    farthest = lax.rem(z + 4, ZS) // 2
    last_half = jnp.where(
        source, jnp.where(farthest == y, 1, 2), jnp.where(away_0 == y, 1, jnp.where(away_1 == y, 0, 2))
    )
    for d in (1, YS - 1):
        other = lax.rem(y + d, YS)

        @pl.when(last_half == 2)
        def _():
            wait(orecv.at[pl.ds(2 * other, 2)], o_recv.at[other])

        @pl.when(last_half < 2)
        def _():
            wait(orecv.at[2 * other + 1 - last_half], o_recv.at[other])
            wait(lean_in.at[other], l_recv.at[other])
            orecv[2 * other + last_half] = lean_in[other].astype(F32)

    wait(narrow.at[pl.ds(2, 2)], n_recv)
    for h in range(2):
        total = obuf[y * 2 + h]
        for d in (1, YS - 1):
            total = total + orecv[lax.rem(y + d, YS) * 2 + h]
        total = total + narrow[2 + h].astype(F32)
        out_ref[0, :, h * half : (h + 1) * half] = total[:cols]
        out_ref[1, :, h * half : (h + 1) * half] = total[cols:]

    def drain(ref, count, sem):
        wait(ref.at[pl.ds(0, count)], sem)

    drain(first, SCENS - 1, f_send)
    drain(ubuf, ITERS * (SCENS - 1), u_send)
    drain(pair.at[:, 0], ITERS + 1, c_send)

    @pl.when(lax.rem(z + c, 2) == 1)
    def _():
        drain(tbuf, (ITERS + 1) * ZS, t_send)

    @pl.when(lax.rem(z + c, 2) == 0)
    def _():
        drain(tbuf, (ITERS + 1) * (ZS - 2), t_send)

    @pl.when(jnp.logical_not(itself))
    def _():
        drain(sbuf, 2, a_send)

    drain(weight, XS - 1, w_send)
    drain(mraw, XS - 1, m_send)

    @pl.when(source)
    def _():
        drain(sbuf, 16, z_send)
        drain(sbuf, 16, p_send)

    @pl.when(jnp.logical_not(source))
    def _():
        drain(sbuf, 12, z_send)
        drain(sbuf, 16, p_send)

    drain(narrow, 2, n_send)
    def neighbour(m):
        return jnp.where(jnp.logical_or(lax.rem(m - y + YS, YS) == 1, lax.rem(m - y + YS, YS) == 3), 1, 0)

    lean_count = jnp.where(source, neighbour(farthest), neighbour(away_0) + neighbour(away_1))
    for count in range(3):

        @pl.when(lean_count == count)
        def _():
            drain(obuf, 2 * (YS - 2) - count, o_send)
            if count:
                drain(lean_in, count, l_send)


def body(link, leaf_inverse, leaf_rhs, node_rhs, node_diag, parent, tile_mask):
    leaves, width, cols = link.shape
    nodes = node_rhs.shape[0]
    vmem = pl.BlockSpec(memory_space=pltpu.VMEM)
    smem = pl.BlockSpec(memory_space=pltpu.SMEM)
    dma = pltpu.SemaphoreType.DMA
    half = cols // 2
    return pl.pallas_call(
        step_kernel,
        out_shape=(
            pltpu.VMEM((nodes, cols), F32),
            pltpu.VMEM((leaves, width), F32),
            pltpu.VMEM((nodes, cols, cols), F32),
        ),
        in_specs=[smem, smem] + [pl.BlockSpec(memory_space=pl.ANY)] * 2 + [vmem] * 3,
        out_specs=(vmem,) * 3,
        scratch_shapes=[
            pltpu.VMEM((leaves, width, cols), BF16),
            pltpu.VMEM((leaves, width, cols), BF16),
            pltpu.VMEM((SCENS, 2 * nodes, cols), F32),
            pltpu.VMEM((ITERS * SCENS, nodes, cols), F32),
            pltpu.VMEM(((ITERS + 1) * ZS, leaves, width), F32),
            pltpu.VMEM((ITERS + 1, 2, leaves, width), F32),
            pltpu.VMEM((2, leaves * width, half), BF16),
            pltpu.VMEM((2 * YS * XS, leaves * width, half), BF16),
            pltpu.VMEM((XS, leaves, cols, width), BF16),
            pltpu.VMEM((XS, 8, 128), F32),
            pltpu.VMEM((XS, nodes * cols, leaves * width), BF16),
            pltpu.VMEM((2 * YS, nodes * cols, half), F32),
            pltpu.VMEM((2 * YS, nodes * cols, half), F32),
            dma, dma, dma, dma((ITERS,)), dma, dma((ITERS + 1,)), dma, dma((ITERS + 1,)),
            dma, dma((2, 2)), dma, dma((XS,)), dma, dma((XS,)), dma, dma((16,)),
            dma, dma((16,)), dma((2, 2)), dma, dma((YS,)),
            pltpu.VMEM((4, nodes * cols, half), BF16), dma, dma,
            pltpu.VMEM((YS, nodes * cols, half), BF16),
            pltpu.VMEM((YS, nodes * cols, half), BF16), dma, dma((YS,)),
            pltpu.VMEM((leaves, width, cols), BF16),
            pltpu.VMEM((leaves, width, width), BF16),
            dma((2,)),
        ],
        compiler_params=pltpu.CompilerParams(collective_id=0, has_side_effects=True, vmem_limit_bytes=60000 * 1024),
        name="step",
    )(parent, tile_mask.reshape(-1), link, leaf_inverse, leaf_rhs, node_rhs, node_diag)


def solution(mesh):
    in_specs = (
        P("scen", None, "blk"),
        P("scen", None, None),
        P("scen", None),
        P(None, "blk"),
        P(None, "blk"),
        P("scen"),
        P("scen", "blk"),
    )
    out_specs = (P(None, "blk"), P("scen", None), P(None, "blk", "scen"))
    return jax.shard_map(body, mesh=mesh, in_specs=in_specs, out_specs=out_specs, check_vma=False)
```

```python
import jax
import jax.numpy as jnp
from jax import lax
from jax.experimental import pallas as pl
from jax.experimental.pallas import tpu as pltpu
from jax.sharding import PartitionSpec as P

ITERS = 4
DAMPING = 0.4
MESH = pl.DeviceIdType.MESH
F32 = jnp.float32
BF16 = jnp.bfloat16
XS = 4
YS = 4
ZS = 8
SCENS = XS * YS


def split_rows(v):
    hi = v.astype(BF16).astype(F32)
    rest = v - hi
    mid = rest.astype(BF16).astype(F32)
    low = rest - mid
    return jnp.concatenate([hi, mid, low, jnp.zeros_like(v)], axis=0).astype(BF16)


def leaf_products(v, mats_ref, contract):
    parts = split_rows(v)
    leaves = mats_ref.shape[0]
    row = lax.broadcasted_iota(jnp.int32, v.shape, 0)
    total = jnp.zeros(v.shape, F32)
    for leaf in range(leaves):
        out = lax.dot_general(
            parts, mats_ref[leaf], (((1,), (contract,)), ((), ())), preferred_element_type=F32
        )
        out = out[0:4] + out[4:8] + out[8:12]
        total = total + jnp.where(row == leaf, out, 0.0)
    return total


def step_kernel(
    parent_ref, mask_ref, link_in, inv_in, rhs_ref, nrhs_ref, ndiag_ref,
    node_ref, leaf_ref, out_ref,
    masked, solved, first, ubuf, tbuf, pair,
    own, sbuf, mraw, weight, mboth, obuf, orecv,
    f_send, f_recv, u_send, u_recv, t_send, t_recv, c_send, c_recv,
    a_send, a_recv, m_send, m_recv, w_send, w_recv, z_send, z_recv,
    p_send, p_recv, q_recv, o_send, o_recv, narrow, n_send, n_recv, lean, lean_in, l_send, l_recv, link_ref, inv_ref, in_sem,
):
    fetch_inv = pltpu.make_async_copy(inv_in, inv_ref, in_sem.at[0])
    fetch_inv.start()
    fetch_link = pltpu.make_async_copy(link_in, link_ref, in_sem.at[1])
    fetch_link.start()
    scen = lax.axis_index("scen")
    blk = lax.axis_index("blk")
    y, x = scen // XS, lax.rem(scen, XS)
    z, c = blk // 2, lax.rem(blk, 2)
    leaves, width, cols = link_ref.shape
    half = cols // 2
    source = lax.rem(z, 2) == x // 2
    partner = (scen, 2 * z + 1 - c)
    barrier = pltpu.get_barrier_semaphore()

    def greet(s, b):
        pl.semaphore_signal(barrier, inc=1, device_id=(s, b), device_id_type=MESH)

    for d in range(1, ZS):
        for e in range(2):
            greet(scen, 2 * lax.rem(z + d, ZS) + e)
    for d in range(1, SCENS):
        greet(lax.rem(scen + d, SCENS), blk)
    for d in range(XS):
        greet(XS * y + lax.rem(x + d, XS), 2 * z + 1 - c)

    def put(src, dst, send, recv, target):
        pltpu.make_async_remote_copy(
            src_ref=src, dst_ref=dst, send_sem=send, recv_sem=recv, device_id=target, device_id_type=MESH
        ).start()

    def wait(ref, sem):
        pltpu.make_async_copy(ref, ref, sem).wait()

    fetch_inv.wait()
    fetch_link.wait()
    for leaf in range(leaves):
        m = link_ref[leaf] * mask_ref[leaf].astype(BF16)
        s = jnp.dot(inv_ref[leaf], m, preferred_element_type=F32).astype(BF16)
        masked[leaf] = m
        solved[leaf] = s
        for h in range(2):
            own[h, leaf * width : (leaf + 1) * width, :] = s[:, h * half : (h + 1) * half]
    owner = [parent_ref[leaf].astype(F32) for leaf in range(leaves)]
    weight[x] = jnp.concatenate(
        [jnp.full((1, 128), owner[leaf], F32) for leaf in range(leaves)] + [jnp.zeros((8 - leaves, 128), F32)],
        axis=0,
    )

    row2 = lax.broadcasted_iota(jnp.int32, nrhs_ref.shape, 0)
    row4 = lax.broadcasted_iota(jnp.int32, rhs_ref.shape, 0)

    def by_parent(rows):
        total = jnp.zeros(nrhs_ref.shape, F32)
        for leaf in range(leaves):
            share_of = jnp.where(row2 == 0, 1.0 - owner[leaf], owner[leaf])
            total = total + share_of * rows[leaf : leaf + 1]
        return total

    def of_parent(values):
        total = jnp.zeros(rhs_ref.shape, F32)
        for leaf in range(leaves):
            mine = values[0:1] * (1.0 - owner[leaf]) + values[1:2] * owner[leaf]
            total = total + jnp.where(row4 == leaf, mine, 0.0)
        return total

    def scen_send(buf, value, send, recv):
        buf[scen] = value
        for d in range(1, SCENS):
            put(buf.at[scen], buf.at[scen], send, recv, (lax.rem(scen + d, SCENS), blk))

    def collect(buf, recv, count):
        wait(buf.at[pl.ds(0, count - 1)], recv)
        total = buf[0]
        for j in range(1, count):
            total = total + buf[j]
        return total

    def blk_begin(it, value):
        pair[it, c] = value
        put(pair.at[it, c], pair.at[it, c], c_send, c_recv.at[it], partner)

    def blk_send(it):
        wait(pair.at[it, 0], c_recv.at[it])
        at = ZS * it + z
        tbuf[at] = pair[it, 0] + pair[it, 1]
        for d in range(1, ZS // 2 + 1):
            to = lax.rem(z + jnp.where(c == 0, ZS - d, d), ZS)

            def both_cores():
                for e in range(2):
                    put(tbuf.at[at], tbuf.at[at], t_send, t_recv.at[it], (scen, 2 * to + e))

            if d < ZS // 2:
                both_cores()
            else:
                pl.when(lax.rem(z + c, 2) == 1)(both_cores)

    def blk_collect(it):
        return collect(tbuf.at[pl.ds(ZS * it, ZS)], t_recv.at[it], ZS)

    def u_at(it):
        return ubuf.at[pl.ds(SCENS * it, SCENS)]

    def piece(m, h, k):
        return (m * 2 + h) * XS + k

    def ring(place, step):
        to = lax.rem(z + jnp.where(c == 0, 1, ZS - 1), ZS)
        put(sbuf.at[place], sbuf.at[place], z_send, z_recv.at[step], (scen, 2 * to + c))

    def share(place, slot):
        put(sbuf.at[place], sbuf.at[place], p_send, slot, partner)

    mine = z // 2

    beside = x + 1 - 2 * lax.rem(x, 2)

    def order(q):
        h = jnp.where(jnp.logical_or(q == 1, q >= 5), 1, 0)
        j = jnp.where(q < 2, 0, jnp.where(q < 5, q - 1, q - 4))
        k = jnp.where(j == 0, x, jnp.where(j == 1, beside, lax.rem(jnp.where(j == 2, beside, x) + 2, XS)))
        return h, k

    def far_order(way, p):
        return jnp.where(way == 0, p, jnp.where(p < 2, p, jnp.where(p < 6, p + 2, p - 4)))

    def crosses(way, p):
        return jnp.logical_and(p >= 2 * way, p < 4 + 2 * way)

    def start_own(begin, end):
        @pl.when(source)
        def _():
            for q in range(begin, end):
                h, k = order(q)
                place = piece(mine, h, k)
                direct = k // 2 == c

                @pl.when(direct)
                def _():
                    wait(sbuf.at[place], a_recv.at[h, lax.rem(k, 2)])
                    ring(place, q)
                    share(place, q_recv.at[h, lax.rem(k, 2)])

                @pl.when(jnp.logical_not(direct))
                def _():
                    wait(sbuf.at[place], q_recv.at[h, lax.rem(k, 2)])
                    ring(place, q)

    def arrival(way, n):
        far = n // 8
        p = lax.rem(n, 8)
        away = jnp.where(source, 2, 1) + 2 * far
        at = lax.rem(z + jnp.where(way == 0, ZS - away, away), ZS)
        h, k = order(jnp.where(far == 0, p, far_order(way, p)))
        comes = jnp.logical_or(jnp.logical_not(source), jnp.logical_or(far == 0, crosses(way, p)))
        return piece(at // 2, h, k), at // 2, comes

    def serve(plain_range, source_range):
        begin = jnp.where(source, source_range[0], plain_range[0])
        end = jnp.where(source, source_range[1], plain_range[1])

        def one(n, carry):
            place, at, comes = arrival(c, n)
            far = n // 8
            p = lax.rem(n, 8)

            @pl.when(comes)
            def _():
                wait(sbuf.at[place], z_recv.at[n])

                @pl.when(jnp.logical_and(jnp.logical_not(source), jnp.logical_or(far == 0, crosses(c, p))))
                def _():
                    ring(place, n)

                @pl.when(jnp.logical_and(source, far == 0))
                def _():
                    @pl.when(jnp.logical_or(c == 0, p < 2))
                    def _():
                        ring(place, n + 8)

                    @pl.when(jnp.logical_and(c == 1, p >= 4))
                    def _():
                        ring(place, n + 6)

                    @pl.when(jnp.logical_and(c == 1, p == 7))
                    def _():
                        for q in (2, 3):
                            ring(piece(at, *order(q)), 12 + q)

                share(place, p_recv.at[n])

            return carry

        lax.fori_loop(begin, end, one, 0)

    def shared(plain_range, source_range):
        begin = jnp.where(source, source_range[0], plain_range[0])
        end = jnp.where(source, source_range[1], plain_range[1])

        def one(n, carry):
            place, at, comes = arrival(1 - c, n)

            @pl.when(comes)
            def _():
                wait(sbuf.at[place], p_recv.at[n])

            return carry

        lax.fori_loop(begin, end, one, 0)

    def product(m, halves):
        def over(k, carry):
            right = [sbuf[piece(m, h, k)] for h in halves]
            right = right[0] if len(right) == 1 else jnp.concatenate(right, axis=1)
            out = jnp.dot(mboth[k], right, preferred_element_type=F32)
            for i, h in enumerate(halves):
                part = out[:, i * half : (i + 1) * half]
                obuf[m * 2 + h] = jnp.where(k == 0, part, obuf[m * 2 + h] + part)
            return carry

        lax.fori_loop(0, XS, over, 0)

    across = lax.rem(y + 2, YS)

    def ship(m, halves):
        @pl.when(jnp.logical_and(m != y, m != across))
        def _():
            for h in halves:
                put(obuf.at[m * 2 + h], orecv.at[y * 2 + h], o_send, o_recv.at[y], (XS * m + x, blk))

        @pl.when(m == across)
        def _():
            for h in halves:
                narrow[h] = obuf[m * 2 + h].astype(BF16)
                put(narrow.at[h], narrow.at[2 + h], n_send, n_recv, (XS * m + x, blk))

    def leaves_by(m):
        away = lax.rem(m - y + YS, YS)
        up = jnp.logical_or(away == 1, jnp.logical_and(away == 2, lax.rem(y, 2) == 0))
        return jnp.where(away == 0, 0, jnp.where(up, 1, 2))

    def near(way):
        away = jnp.where(source, 2, 1)
        return lax.rem(z + (ZS - away if way == 0 else away), ZS) // 2

    def free_for(way):
        link = leaves_by(near(way))
        taken = jnp.logical_and(source, link == leaves_by(mine))
        if way == 1:
            taken = jnp.logical_or(taken, link == leaves_by(near(0)))
        return jnp.logical_not(taken)

    def ship_early(way, at_source=True):
        @pl.when(jnp.logical_and(free_for(way), jnp.logical_or(at_source, jnp.logical_not(source))))
        def _():
            ship(near(way), (0,))

    def ship_own_late():
        @pl.when(source)
        def _():
            ship(mine, (1,))

    def ship_late(way, at_source=True):
        @pl.when(jnp.logical_not(jnp.logical_and(free_for(way), jnp.logical_or(at_source, jnp.logical_not(source)))))
        def _():
            ship(near(way), (0,))

        ship(near(way), (1,))

    def finish_own():
        @pl.when(source)
        def _():
            product(mine, (0, 1))
            ship(mine, (0,))

    def far_halves(i, act):
        def one(way, carry):
            m = lax.rem(z + jnp.where(way == 0, ZS - 3, 3), ZS) // 2

            @pl.when(jnp.logical_not(source))
            def _():
                for h in range(2):
                    @pl.when(way == (i + h) % 2)
                    def _():
                        act(m, (h,))

            return carry

        lax.fori_loop(0, 2, one, 0)

        @pl.when(source)
        def _():
            act(lax.rem(z + 4, ZS) // 2, (i,))

    def both_acts(m, halves):
        product(m, halves)
        ship(m, halves)

    def last_acts(m, halves):
        product(m, halves)
        h = halves[0]

        @pl.when(m != y)
        def _():
            lean[lax.rem(m - y + YS, YS)] = obuf[m * 2 + h].astype(BF16)

        @pl.when(m == across)
        def _():
            put(lean.at[2], narrow.at[2 + h], n_send, n_recv, (XS * m + x, blk))

        @pl.when(jnp.logical_and(m != y, m != across))
        def _():
            put(lean.at[lax.rem(m - y + YS, YS)], lean_in.at[y], l_send, l_recv.at[y], (XS * m + x, blk))

    def spread(begin, end):
        for leaf in range(begin, end):
            for d in (1, 3, 2):
                put(mraw.at[x, leaf], mraw.at[x, leaf], m_send, m_recv.at[x], (XS * y + lax.rem(x + d, XS), blk))

    def turn():
        for leaf in range(leaves):
            mraw[x, leaf] = masked[leaf].astype(F32).T.astype(BF16)

    def gathered():
        for d in range(1, XS):
            other = lax.rem(x + d, XS)
            wait(weight.at[other], w_recv.at[other])
            wait(mraw.at[other], m_recv.at[other])

        def both(k, carry):
            w = weight[k]
            for leaf in range(leaves):
                row = jnp.concatenate([w[leaf : leaf + 1]] * (width // 128), axis=1).astype(BF16)
                raw = mraw[k, leaf]
                span = slice(leaf * width, (leaf + 1) * width)
                mboth[k, :cols, span] = raw * (1 - row)
                mboth[k, cols:, span] = raw * row
            return carry

        lax.fori_loop(0, XS, both, 0)

    leaf_rhs = rhs_ref[...]
    leaf_solve = leaf_products(leaf_rhs, inv_ref, 1)
    rhs_terms = by_parent(leaf_products(leaf_solve, masked, 0))
    diag_rows = jnp.concatenate(
        [
            jnp.sum(masked[leaf].astype(F32) * solved[leaf].astype(F32), axis=0, keepdims=True)
            for leaf in range(leaves)
        ],
        axis=0,
    )
    opening = jnp.concatenate([rhs_terms, by_parent(diag_rows)], axis=0)
    pl.semaphore_wait(barrier, 2 * (ZS - 1) + (SCENS - 1) + XS)

    scen_send(first, opening, f_send, f_recv)

    to_x = 2 * lax.rem(z, 2) + c
    lane = x // 2
    itself = jnp.logical_and(to_x == x, lane == c)
    for h in range(2):
        place = piece(mine, h, x)
        slot = a_recv.at[h, lax.rem(x, 2)]

        @pl.when(itself)
        def _():
            pltpu.make_async_copy(own.at[h], sbuf.at[place], slot).start()

        @pl.when(jnp.logical_not(itself))
        def _():
            put(own.at[h], sbuf.at[place], a_send, slot, (XS * y + to_x, 2 * z + lane))

    for d in (1, 3, 2):
        put(weight.at[x], weight.at[x], w_send, w_recv.at[x], (XS * y + lax.rem(x + d, XS), blk))

    start_own(0, 2)
    sums = collect(first, f_recv, SCENS)
    node_diag = ndiag_ref[...]
    reduced = nrhs_ref[...] - sums[0:2]
    scaling = node_diag + sums[2:4]
    state = reduced / scaling

    def sweep_a(it, value):
        blk_begin(it, leaf_products(of_parent(value), solved, 1))

    def sweep_b(it):
        inner = blk_collect(it)
        scen_send(u_at(it), by_parent(leaf_products(inner, masked, 0)), u_send, u_recv.at[it])

    def sweep_c(it, value):
        product_of = node_diag * value + collect(u_at(it), u_recv.at[it], SCENS)
        return value + DAMPING * (reduced - product_of) / scaling

    sweep_a(0, state)
    turn()
    blk_send(0)
    start_own(2, 5)
    sweep_b(0)
    spread(0, 2)
    start_own(5, 8)
    serve((0, 2), (0, 0))
    state = sweep_c(0, state)
    sweep_a(1, state)
    serve((2, 4), (0, 0))
    blk_send(1)
    serve((4, 5), (0, 0))
    sweep_b(1)
    spread(2, 4)
    serve((5, 7), (0, 2))
    state = sweep_c(1, state)
    sweep_a(2, state)
    serve((7, 8), (2, 5))
    blk_send(2)
    serve((8, 9), (5, 6))
    sweep_b(2)
    gathered()
    finish_own()
    serve((9, 11), (6, 8))
    shared((0, 8), (0, 8))
    product(near(0), (0, 1))
    ship_early(0)
    state = sweep_c(2, state)
    sweep_a(3, state)
    serve((11, 12), (8, 8))
    blk_send(3)
    product(near(1), (0, 1))
    ship_early(1)
    serve((12, 14), (8, 12))
    shared((8, 14), (8, 12))
    sweep_b(3)
    far_halves(0, both_acts)
    ship_own_late()
    ship_late(0)
    ship_late(1)
    serve((14, 16), (12, 14))
    shared((14, 16), (12, 14))
    far_halves(1, last_acts)
    state = sweep_c(3, state)
    node_ref[...] = state
    blk_begin(ITERS, leaf_products(of_parent(state), masked, 1))
    blk_send(ITERS)
    coupling = blk_collect(ITERS)
    leaf_ref[...] = leaf_products(leaf_rhs - coupling, inv_ref, 1)

    away_0 = lax.rem(z + ZS - 3, ZS) // 2
    away_1 = lax.rem(z + 3, ZS) // 2
    farthest = lax.rem(z + 4, ZS) // 2
    last_half = jnp.where(
        source, jnp.where(farthest == y, 1, 2), jnp.where(away_0 == y, 1, jnp.where(away_1 == y, 0, 2))
    )
    for d in (1, YS - 1):
        other = lax.rem(y + d, YS)

        @pl.when(last_half == 2)
        def _():
            wait(orecv.at[pl.ds(2 * other, 2)], o_recv.at[other])

        @pl.when(last_half < 2)
        def _():
            wait(orecv.at[2 * other + 1 - last_half], o_recv.at[other])
            wait(lean_in.at[other], l_recv.at[other])
            orecv[2 * other + last_half] = lean_in[other].astype(F32)

    wait(narrow.at[pl.ds(2, 2)], n_recv)
    for h in range(2):
        total = obuf[y * 2 + h]
        for d in (1, YS - 1):
            total = total + orecv[lax.rem(y + d, YS) * 2 + h]
        total = total + narrow[2 + h].astype(F32)
        out_ref[0, :, h * half : (h + 1) * half] = total[:cols]
        out_ref[1, :, h * half : (h + 1) * half] = total[cols:]

    def drain(ref, count, sem):
        wait(ref.at[pl.ds(0, count)], sem)

    drain(first, SCENS - 1, f_send)
    drain(ubuf, ITERS * (SCENS - 1), u_send)
    drain(pair.at[:, 0], ITERS + 1, c_send)

    @pl.when(lax.rem(z + c, 2) == 1)
    def _():
        drain(tbuf, (ITERS + 1) * ZS, t_send)

    @pl.when(lax.rem(z + c, 2) == 0)
    def _():
        drain(tbuf, (ITERS + 1) * (ZS - 2), t_send)

    @pl.when(jnp.logical_not(itself))
    def _():
        drain(sbuf, 2, a_send)

    drain(weight, XS - 1, w_send)
    drain(mraw, XS - 1, m_send)

    @pl.when(source)
    def _():
        drain(sbuf, 16, z_send)
        drain(sbuf, 16, p_send)

    @pl.when(jnp.logical_not(source))
    def _():
        drain(sbuf, 12, z_send)
        drain(sbuf, 16, p_send)

    drain(narrow, 2, n_send)
    def neighbour(m):
        return jnp.where(jnp.logical_or(lax.rem(m - y + YS, YS) == 1, lax.rem(m - y + YS, YS) == 3), 1, 0)

    lean_count = jnp.where(source, neighbour(farthest), neighbour(away_0) + neighbour(away_1))
    for count in range(3):

        @pl.when(lean_count == count)
        def _():
            drain(obuf, 2 * (YS - 2) - count, o_send)
            if count:
                drain(lean_in, count, l_send)


def body(link, leaf_inverse, leaf_rhs, node_rhs, node_diag, parent, tile_mask):
    leaves, width, cols = link.shape
    nodes = node_rhs.shape[0]
    vmem = pl.BlockSpec(memory_space=pltpu.VMEM)
    smem = pl.BlockSpec(memory_space=pltpu.SMEM)
    dma = pltpu.SemaphoreType.DMA
    half = cols // 2
    return pl.pallas_call(
        step_kernel,
        out_shape=(
            pltpu.VMEM((nodes, cols), F32),
            pltpu.VMEM((leaves, width), F32),
            pltpu.VMEM((nodes, cols, cols), F32),
        ),
        in_specs=[smem, smem] + [pl.BlockSpec(memory_space=pl.ANY)] * 2 + [vmem] * 3,
        out_specs=(vmem,) * 3,
        scratch_shapes=[
            pltpu.VMEM((leaves, width, cols), BF16),
            pltpu.VMEM((leaves, width, cols), BF16),
            pltpu.VMEM((SCENS, 2 * nodes, cols), F32),
            pltpu.VMEM((ITERS * SCENS, nodes, cols), F32),
            pltpu.VMEM(((ITERS + 1) * ZS, leaves, width), F32),
            pltpu.VMEM((ITERS + 1, 2, leaves, width), F32),
            pltpu.VMEM((2, leaves * width, half), BF16),
            pltpu.VMEM((2 * YS * XS, leaves * width, half), BF16),
            pltpu.VMEM((XS, leaves, cols, width), BF16),
            pltpu.VMEM((XS, 8, 128), F32),
            pltpu.VMEM((XS, nodes * cols, leaves * width), BF16),
            pltpu.VMEM((2 * YS, nodes * cols, half), F32),
            pltpu.VMEM((2 * YS, nodes * cols, half), F32),
            dma, dma, dma, dma((ITERS,)), dma, dma((ITERS + 1,)), dma, dma((ITERS + 1,)),
            dma, dma((2, 2)), dma, dma((XS,)), dma, dma((XS,)), dma, dma((16,)),
            dma, dma((16,)), dma((2, 2)), dma, dma((YS,)),
            pltpu.VMEM((4, nodes * cols, half), BF16), dma, dma,
            pltpu.VMEM((YS, nodes * cols, half), BF16),
            pltpu.VMEM((YS, nodes * cols, half), BF16), dma, dma((YS,)),
            pltpu.VMEM((leaves, width, cols), BF16),
            pltpu.VMEM((leaves, width, width), BF16),
            dma((2,)),
        ],
        compiler_params=pltpu.CompilerParams(collective_id=0, has_side_effects=True, vmem_limit_bytes=60000 * 1024),
        name="step",
    )(parent, tile_mask.reshape(-1), link, leaf_inverse, leaf_rhs, node_rhs, node_diag)


def solution(mesh):
    in_specs = (
        P("scen", None, "blk"),
        P("scen", None, None),
        P("scen", None),
        P(None, "blk"),
        P(None, "blk"),
        P("scen"),
        P("scen", "blk"),
    )
    out_specs = (P(None, "blk"), P("scen", None), P(None, "blk", "scen"))
    return jax.shard_map(body, mesh=mesh, in_specs=in_specs, out_specs=out_specs, check_vma=False)
```
